512 devices in a mesh: tm: 16 (over z_lo, core), tmpl: 32 (over z_hi, y, x).
Axes of the slice: x: 4, y: 4, z: 16 (z_hi: 2, z_lo: 8; z = z_hi * 8 + z_lo), core: 2. Of those that a mesh axis runs over, the one named last changes fastest.
Arguments:
- waveforms: bfloat16 [3072, 3, 12288], P('tmpl', None, 'tm'), may hold values from -360 to 360
- templates: bfloat16 [32, 16, 48, 600], P('tmpl', 'tm'), may hold values from -6 to 6
- group_stations: int32 [32, 16], replicated, may hold values from 0 to 3071, as said below
- template_rows: int32 [32, 16, 16], P('tmpl'), may hold values from 0 to 15, as said below
- moveouts: int32 [32, 16, 16], P('tmpl'), may hold values from 0 to 127, as said below
Outputs:
- network_stack: float32 [32, 16, 12288], P('tmpl', None, 'tm')
The draws below stay inside these ranges and needn't reach their ends.
Inputs may be any that keep to these rules, and one draw needn't show every extreme that they name: `group_stations`: A group's stations are distinct; at most 2 of them have the same station id // 96, and in every group some value of station id // 96 is shared by exactly 2 of them. `template_rows`: A template's 16 entries are distinct, and every position of a group's table is named by exactly 16 of the group's templates. `moveouts`: in every template some station has moveout 0 and another has 127.
All inputs are finite; a program needn't handle non-finite values.
Results may differ from the reference program's by a relative error of at most 0.0059.
Values may be sent and summed in bfloat16 or wider, within the bound.
A program may use at most 64 MiB of HBM per device.

```python
import math
import jax
import jax.numpy as jnp
from jax import lax

STA_DEV = 96
L = 600
K = 16
GS = 16
TPL_DEV = 16
OFFMAX = 128
USES = 16
GROUPS = 32
CAP = 2
STATIONS = 3072
NT = 12288


def draw_waveforms(key, part):
    first_key, second_key, third_key, dead_key = jax.random.split(key, 4)
    noise = jax.random.truncated_normal(first_key, -4.0, 4.0, (STATIONS, 3, NT), jnp.float32)
    level = jnp.exp(jax.random.uniform(second_key, (STATIONS, 3, 1), jnp.float32, 0.0, math.log(10.0)))
    envelope = jnp.exp(jax.random.uniform(third_key, (STATIONS, 1, NT // 64, 1), jnp.float32, 0.0, math.log(3.0)))
    envelope = jnp.broadcast_to(envelope, (STATIONS, 1, NT // 64, 64)).reshape(STATIONS, 1, NT)
    dead = jax.random.bernoulli(dead_key, 0.125, (STATIONS, 3, 1))
    return jnp.where(dead, 0.01 * noise, noise * level * envelope).astype(jnp.bfloat16)


def draw_group_stations(key, part):

    def one_group(group_key):
        owner_key, pool_key, order_key, local_key = jax.random.split(group_key, 4)
        first_owner = jax.random.randint(owner_key, (), 0, GROUPS)
        others = (first_owner + 1 + jnp.arange(GROUPS - 1, dtype=jnp.int32)) % GROUPS
        pooled = jax.random.permutation(pool_key, jnp.tile(others, CAP))
        owners = jnp.concatenate([jnp.full((CAP,), first_owner, jnp.int32), pooled[:GS - CAP]])
        owners = jax.random.permutation(order_key, owners)
        position = jnp.arange(GS, dtype=jnp.int32)
        same_owner = owners[:, None] == owners[None, :]
        earlier = position[:, None] > position[None, :]
        owner_rank = jnp.sum((same_owner & earlier).astype(jnp.int32), axis=1)
        station_perms = jax.vmap(lambda sub_key: jax.random.permutation(sub_key, STA_DEV))(jax.random.split(local_key, GROUPS))
        row_local = station_perms[owners, owner_rank]
        return owners * STA_DEV + row_local
    return jax.vmap(one_group)(jax.random.split(key, GROUPS)).astype(jnp.int32)


def draw_template_rows(key, part):

    def one_group(group_key):
        phase_key, class_key, pick_key = jax.random.split(group_key, 3)
        phase_of = jax.random.permutation(phase_key, TPL_DEV)
        class_of = jax.random.permutation(class_key, GS) % TPL_DEV
        member = (phase_of[:, None] - class_of[None, :]) % TPL_DEV < USES

        def one_template(template_key, member_row):
            scores = jax.random.permutation(template_key, GS) + jnp.where(member_row, 0, GS)
            return jnp.argsort(scores, stable=True)[:K]
        return jax.vmap(one_template)(jax.random.split(pick_key, TPL_DEV), member)
    return jax.vmap(one_group)(jax.random.split(key, GROUPS)).astype(jnp.int32)


def draw_moveouts(key, part):
    raw_key, first_key, last_key = jax.random.split(key, 3)
    raw_values = jax.random.randint(raw_key, (GROUPS, TPL_DEV, K), 0, OFFMAX)
    earliest = jax.random.randint(first_key, (GROUPS, TPL_DEV, 1), 0, K)
    latest = (earliest + 1 + jax.random.randint(last_key, (GROUPS, TPL_DEV, 1), 0, K - 1)) % K
    slot_ids = jnp.arange(K, dtype=jnp.int32)
    result = jnp.where(slot_ids == earliest, 0, jnp.where(slot_ids == latest, OFFMAX - 1, raw_values))
    return result.astype(jnp.int32)


def level_of(own_key, shape, cuts, least, top_value):
    factor_of = 1.0
    for dim, parts in cuts:
        heights = jax.random.uniform(jax.random.fold_in(jax.random.fold_in(own_key, 6), dim), (parts,), jnp.float32, least / len(cuts), top_value / len(cuts))
        factor_of = factor_of * jnp.repeat(jnp.exp(heights), shape[dim] // parts).reshape((-1,) + (1,) * (len(shape) - 1 - dim))
    return factor_of


def gaussian(own_key, dims, scale, most, cuts=(), kind=jnp.bfloat16):
    array = scale * jax.random.normal(own_key, dims, jnp.float32)
    if cuts:
        array = array * level_of(own_key, dims, cuts, -0.22, 0.18)
    return jnp.clip(array, -most, most).astype(kind)


def setup_inputs(seed: int = 0) -> dict:
    arg_keys = jax.random.split(jax.random.key(seed), 6)
    waveforms = draw_waveforms(jax.random.fold_in(arg_keys[5], 71), 0)
    templates = gaussian(arg_keys[1], (GROUPS, TPL_DEV, K * 3, L), 1.0, 6.0, ((0, 32), (1, 16)))
    group_stations = draw_group_stations(jax.random.fold_in(arg_keys[5], 71), 0)
    template_rows = draw_template_rows(jax.random.fold_in(arg_keys[5], 71), 0)
    moveouts = draw_moveouts(jax.random.fold_in(arg_keys[5], 71), 0)
    return dict(waveforms=waveforms, templates=templates, group_stations=group_stations, template_rows=template_rows, moveouts=moveouts)


def normalize(raw):
    values = raw.astype(jnp.float32)
    centred = values - lax.optimization_barrier(jnp.mean(values, axis=-1, keepdims=True))
    factor = lax.rsqrt(lax.optimization_barrier(jnp.sum(centred * centred, axis=-1, keepdims=True)) + 1e-06)
    return (centred * factor).astype(jnp.bfloat16)

def reference(waveforms, templates, group_stations, template_rows, moveouts):
    samples = waveforms.shape[2]
    padded_taps = (L + 127) // 128 * 128
    extent = OFFMAX + padded_taps
    span_width = samples + OFFMAX
    length = samples + extent
    fft_size = 1 << (length - 1).bit_length()
    normed = normalize(templates).astype(jnp.float32).reshape(GROUPS, TPL_DEV, K, 3, L)

    def one_group(group):
        station_ids = group_stations[group]
        rows_data = jnp.take(waveforms, station_ids, axis=0).astype(jnp.float32)
        rows_data = jnp.pad(rows_data, ((0, 0), (0, 0), (0, extent)))
        zeros_col = jnp.zeros((GS, 3, 1), jnp.float32)
        running = jnp.concatenate([zeros_col, jnp.cumsum(rows_data, axis=2)], axis=2)
        running_sq = jnp.concatenate([zeros_col, jnp.cumsum(rows_data * rows_data, axis=2)], axis=2)
        window_sum = running[:, :, L:L + span_width] - running[:, :, :span_width]
        window_sq = running_sq[:, :, L:L + span_width] - running_sq[:, :, :span_width]
        spread = jnp.sqrt(jnp.maximum(window_sq - window_sum * window_sum / L, 1.0))
        spectra = jnp.fft.rfft(rows_data, n=fft_size, axis=-1)

        def one_template(index):
            members = template_rows[group, index]
            delays = moveouts[group, index]
            filters = jnp.fft.rfft(normed[group, index], n=fft_size, axis=-1)
            correl = jnp.fft.irfft(spectra[members] * jnp.conj(filters), n=fft_size, axis=-1)[:, :, :span_width]
            ratios = lax.optimization_barrier(jnp.sum(correl / spread[members], axis=1))
            pieces = jax.vmap(lambda series, delay: lax.dynamic_slice_in_dim(series, delay, samples))(ratios, delays)
            return lax.optimization_barrier(jnp.sum(pieces, axis=0))
        return lax.map(one_template, jnp.arange(TPL_DEV, dtype=jnp.int32))
    return lax.map(one_group, jnp.arange(GROUPS, dtype=jnp.int32))
```

```python
import functools

import jax
import jax.numpy as jnp
from jax import lax
from jax.experimental import pallas as pl
from jax.experimental.pallas import tpu as pltpu
from jax.sharding import PartitionSpec as P

STRIDE = 8
LANES = 128


def iota(shape, dim):
    return lax.broadcasted_iota(jnp.int32, shape, dim)


def correlate_kernel(taps, rowidx, delays, rec_ref, tpl_ref, out_ref, tplf, xa, xb, inv, zs, ws, acc):
    stations = rowidx.shape[0]
    tpls = rowidx.shape[1]
    channels = xa.shape[0] // stations
    nrc = xa.shape[0]
    samples = rec_ref.shape[1]
    frames = samples // STRIDE
    padded = tpl_ref.shape[1]
    kblocks = padded // LANES
    groups = taps // STRIDE + 1
    lane = iota((STRIDE, LANES), 1)
    sub = iota((STRIDE, LANES), 0)

    tplf[...] = tpl_ref[...].astype(jnp.float32)

    gap = iota((samples, LANES), 0) - STRIDE * iota((samples, LANES), 1)
    flat_lane = iota((nrc, LANES), 1)
    for e in range(STRIDE):
        pick = jnp.where(gap == e, 1.0, 0.0).astype(jnp.bfloat16)
        phase = jnp.dot(rec_ref[...], pick, preferred_element_type=jnp.float32)
        later = pltpu.roll(phase[nrc:], frames, axis=1)
        xa[:, e, :] = jnp.where(flat_lane < frames, phase[:nrc], later)
        xb[:, e, :] = later

    ahead = iota((2 * LANES, LANES), 0) - iota((2 * LANES, LANES), 1)
    band = jnp.where((ahead >= 0) & (ahead < taps // STRIDE), 1.0, 0.0).astype(jnp.bfloat16)
    flat = jnp.concatenate([xa[...].reshape(nrc * STRIDE, LANES), xb[...].reshape(nrc * STRIDE, LANES)], axis=1)
    square = flat * flat
    high = square.astype(jnp.bfloat16)
    low = (square - high.astype(jnp.float32)).astype(jnp.bfloat16)

    def banded(v):
        return jnp.dot(v, band, preferred_element_type=jnp.float32)

    def octet(v):
        v = v.reshape(nrc, STRIDE, LANES)
        row = iota((nrc, STRIDE, LANES), 1)
        for k in (1, 2, 4):
            nxt = pltpu.roll(v, LANES - 1, axis=2)
            v = v + pltpu.roll(jnp.where(row < k, nxt, v), STRIDE - k, axis=1)
        return v

    wsum = octet(banded(flat.astype(jnp.bfloat16)))
    wsq = octet(banded(high) + banded(low))
    inv[...] = lax.rsqrt(jnp.maximum(wsq - wsum * wsum / taps, 1.0))

    acc[...] = jnp.zeros_like(acc)
    for i in range(groups, padded // STRIDE, 2):
        for c in range(channels):
            zs[c, STRIDE * i : STRIDE * (i + 2), :] = jnp.zeros((2 * STRIDE, LANES), jnp.bfloat16)

    def station(r, carry):
        ratio = None
        for c in range(channels):
            rc = r * channels + c
            a, b = xa[rc], xb[rc]
            for i in range(0, groups, 2):
                pair = [
                    pltpu.roll(jnp.where(lane < s, b, a), (LANES - s) % LANES, axis=1) for s in (i, i + 1)
                ]
                zs[c, STRIDE * i : STRIDE * (i + 2), :] = jnp.concatenate(pair, axis=0).astype(jnp.bfloat16)
            for t in range(0, tpls, 2):
                rolled = []
                for tt in (t, t + 1):
                    row = tplf[pl.ds(rowidx[r, tt] + c, 1), :]
                    parts = [
                        pltpu.roll(
                            jnp.broadcast_to(row[:, LANES * k : LANES * (k + 1)], (STRIDE, LANES)),
                            0, axis=1, stride=1, stride_axis=0,
                        )
                        for k in range(kblocks)
                    ]
                    rolled.append(parts)
                for k in range(kblocks):
                    both = [
                        jnp.where(lane < sub, p[k - 1] if k else jnp.zeros_like(p[0]), p[k]) for p in rolled
                    ]
                    ws[c, STRIDE * t : STRIDE * (t + 2), LANES * k : LANES * (k + 1)] = jnp.concatenate(
                        both, axis=0
                    ).astype(jnp.bfloat16)
            numer = jnp.dot(ws[c], zs[c], preferred_element_type=jnp.float32)
            part = numer.reshape(tpls, STRIDE, LANES) * inv[rc][None]
            ratio = part if ratio is None else ratio + part
        for t in range(tpls):
            m = delays[r, t]
            f = m // STRIDE
            e = m - f * STRIDE
            near = pltpu.roll(ratio[t], (LANES - f) % LANES, axis=1)
            far = pltpu.roll(near, LANES - 1, axis=1)
            acc[t] += pltpu.roll(jnp.where(sub < e, far, near), (STRIDE - e) % STRIDE, axis=0)
        return carry

    lax.fori_loop(0, stations, station, 0)

    total = acc[...].reshape(tpls * STRIDE, LANES)
    p1 = total.astype(jnp.bfloat16)
    rest = total - p1.astype(jnp.float32)
    p2 = rest.astype(jnp.bfloat16)
    p3 = (rest - p2.astype(jnp.float32)).astype(jnp.bfloat16)
    spots = iota((LANES, samples), 1) // STRIDE
    spread_out = jnp.where(spots == iota((LANES, samples), 0), 1.0, 0.0).astype(jnp.bfloat16)

    def placed(v):
        return jnp.dot(v, spread_out, preferred_element_type=jnp.float32)

    wide = (placed(p1) + placed(p2) + placed(p3)).reshape(tpls, STRIDE, samples)
    mine = iota((tpls, STRIDE, samples), 2) % STRIDE == iota((tpls, STRIDE, samples), 1)
    out_ref[...] = jnp.sum(jnp.where(mine, wide, 0.0), axis=1)


def correlate(rec, tpl, rowidx, delays, taps):
    stations, tpls = rowidx.shape
    nrc = rec.shape[0] // 2
    samples = rec.shape[1]
    padded = tpl.shape[1]
    channels = nrc // stations
    vm = pl.BlockSpec(memory_space=pltpu.VMEM)
    sm = pl.BlockSpec(memory_space=pltpu.SMEM)
    return pl.pallas_call(
        functools.partial(correlate_kernel, taps),
        out_shape=jax.ShapeDtypeStruct((tpls, samples), jnp.float32),
        in_specs=[sm, sm, vm, vm],
        out_specs=vm,
        scratch_shapes=[
            pltpu.VMEM(tpl.shape, jnp.float32),
            pltpu.VMEM((nrc, STRIDE, LANES), jnp.float32),
            pltpu.VMEM((nrc, STRIDE, LANES), jnp.float32),
            pltpu.VMEM((nrc, STRIDE, LANES), jnp.float32),
            pltpu.VMEM((channels, padded, LANES), jnp.bfloat16),
            pltpu.VMEM((channels, tpls * STRIDE, padded), jnp.bfloat16),
            pltpu.VMEM((tpls, STRIDE, LANES), jnp.float32),
        ],
        compiler_params=pltpu.CompilerParams(vmem_limit_bytes=32 << 20),
    )(rowidx, delays, rec, tpl)


def normalize(raw):
    values = raw.astype(jnp.float32)
    centred = values - jnp.mean(values, axis=-1, keepdims=True)
    factor = lax.rsqrt(jnp.sum(centred * centred, axis=-1, keepdims=True) + 1e-06)
    return (centred * factor).astype(jnp.bfloat16)


def fetch_rows(source, group_stations, capacity, own_index):
    groups, table_size = group_stations.shape
    station_count = source.shape[0]
    owners = group_stations // station_count
    row_local = group_stations % station_count
    position = jnp.arange(table_size, dtype=jnp.int32)
    same_owner = owners[:, :, None] == owners[:, None, :]
    earlier = position[:, None] > position[None, :]
    owner_rank = jnp.sum((same_owner & earlier[None]).astype(jnp.int32), axis=2)
    slot_ids = jnp.arange(capacity, dtype=jnp.int32)
    matched = (owners[:, :, None] == own_index) & (
        owner_rank[:, :, None] == slot_ids[None, None, :]
    )
    picked = jnp.sum(jnp.where(matched, row_local[:, :, None], 0), axis=1)
    outgoing = jnp.take(source, picked.reshape(-1), axis=0)
    outgoing = outgoing.reshape(groups, capacity, source.shape[1], source.shape[2])
    incoming = lax.all_to_all(outgoing, "tmpl", split_axis=0, concat_axis=0, tiled=True)
    arrived = incoming.reshape(groups * capacity, source.shape[1], source.shape[2])
    mine_owner = jnp.take(owners, own_index, axis=0)
    mine_rank = jnp.take(owner_rank, own_index, axis=0)
    return jnp.take(arrived, mine_owner * capacity + mine_rank, axis=0)


def per_device(waveforms, templates, group_stations, template_rows, moveouts):
    groups = lax.axis_size("tmpl")
    windows = lax.axis_size("tm")
    own_index = lax.axis_index("tmpl")
    channels, samples = waveforms.shape[1:]
    table_size = group_stations.shape[1]
    capacity = max(2, 2 * table_size // groups)
    taps = templates.shape[3]
    padded = (taps + LANES - 1) // LANES * LANES
    normed = normalize(templates[0, 0])
    normed = jnp.pad(normed, ((0, 0), (0, padded - taps)))
    tpl = lax.all_gather(normed, "tm", axis=0, tiled=True)
    rows = fetch_rows(waveforms, group_stations, capacity, own_index)
    rows = rows.reshape(table_size * channels, samples)
    later = lax.ppermute(rows, "tm", [(w, w - 1) for w in range(1, windows)])
    rec = jnp.concatenate([rows, later], axis=0)
    lists, shifts = template_rows[0], moveouts[0]
    tpls, per_template = lists.shape
    hit = lists[:, :, None] == jnp.arange(table_size, dtype=jnp.int32)
    slot = jnp.sum(jnp.where(hit, jnp.arange(per_template, dtype=jnp.int32)[None, :, None], 0), axis=1)
    delays = jnp.sum(jnp.where(hit, shifts[:, :, None], 0), axis=1)
    base = jnp.arange(tpls, dtype=jnp.int32)[:, None] * (per_template * channels)
    rowidx = base + slot * channels
    return correlate(rec, tpl, rowidx.T, delays.T, taps)[None]


def solution(mesh):
    in_specs = (
        P("tmpl", None, "tm"),
        P("tmpl", "tm", None, None),
        P(),
        P("tmpl", None, None),
        P("tmpl", None, None),
    )
    out_specs = P("tmpl", None, "tm")
    return jax.shard_map(
        per_device, mesh=mesh, in_specs=in_specs, out_specs=out_specs, check_vma=False
    )
```

```python
import functools

import jax
import jax.numpy as jnp
from jax import lax
from jax.experimental import pallas as pl
from jax.experimental.pallas import tpu as pltpu
from jax.sharding import PartitionSpec as P

STRIDE = 8
LANES = 128


def iota(shape, dim):
    return lax.broadcasted_iota(jnp.int32, shape, dim)


def correlate_kernel(taps, rowidx, delays, rec_ref, tpl_ref, out_ref, tplf, xa, xb, inv, zs, ws, acc):
    stations = rowidx.shape[0]
    tpls = rowidx.shape[1]
    channels = xa.shape[0] // stations
    nrc = xa.shape[0]
    samples = rec_ref.shape[1]
    frames = samples // STRIDE
    padded = tpl_ref.shape[1]
    kblocks = padded // LANES
    groups = taps // STRIDE + 1
    lane = iota((STRIDE, LANES), 1)
    sub = iota((STRIDE, LANES), 0)

    tplf[...] = tpl_ref[...].astype(jnp.float32)

    gap = iota((samples, LANES), 0) - STRIDE * iota((samples, LANES), 1)
    flat_lane = iota((nrc, LANES), 1)
    for e in range(STRIDE):
        pick = jnp.where(gap == e, 1.0, 0.0).astype(jnp.bfloat16)
        phase = jnp.dot(rec_ref[...], pick, preferred_element_type=jnp.float32)
        later = pltpu.roll(phase[nrc:], frames, axis=1)
        xa[:, e, :] = jnp.where(flat_lane < frames, phase[:nrc], later)
        xb[:, e, :] = later

    ahead = iota((2 * LANES, LANES), 0) - iota((2 * LANES, LANES), 1)
    band = jnp.where((ahead >= 0) & (ahead < taps // STRIDE), 1.0, 0.0).astype(jnp.bfloat16)
    flat = jnp.concatenate([xa[...].reshape(nrc * STRIDE, LANES), xb[...].reshape(nrc * STRIDE, LANES)], axis=1)
    square = flat * flat
    high = square.astype(jnp.bfloat16)
    low = (square - high.astype(jnp.float32)).astype(jnp.bfloat16)

    def banded(v):
        return jnp.dot(v, band, preferred_element_type=jnp.float32)

    def octet(v):
        v = v.reshape(nrc, STRIDE, LANES)
        row = iota((nrc, STRIDE, LANES), 1)
        for k in (1, 2, 4):
            nxt = pltpu.roll(v, LANES - 1, axis=2)
            v = v + pltpu.roll(jnp.where(row < k, nxt, v), STRIDE - k, axis=1)
        return v

    wsum = octet(banded(flat.astype(jnp.bfloat16)))
    wsq = octet(banded(high) + banded(low))
    inv[...] = lax.rsqrt(jnp.maximum(wsq - wsum * wsum / taps, 1.0))

    acc[...] = jnp.zeros_like(acc)
    for i in range(groups, padded // STRIDE, 2):
        for c in range(channels):
            zs[c, STRIDE * i : STRIDE * (i + 2), :] = jnp.zeros((2 * STRIDE, LANES), jnp.bfloat16)

    def station(r, carry):
        ratio = None
        for c in range(channels):
            rc = r * channels + c
            a, b = xa[rc], xb[rc]
            for i in range(0, groups, 2):
                pair = [
                    pltpu.roll(jnp.where(lane < s, b, a), (LANES - s) % LANES, axis=1) for s in (i, i + 1)
                ]
                zs[c, STRIDE * i : STRIDE * (i + 2), :] = jnp.concatenate(pair, axis=0).astype(jnp.bfloat16)
            for t in range(0, tpls, 2):
                rolled = []
                for tt in (t, t + 1):
                    row = tplf[pl.ds(rowidx[r, tt] + c, 1), :]
                    parts = [
                        pltpu.roll(
                            jnp.broadcast_to(row[:, LANES * k : LANES * (k + 1)], (STRIDE, LANES)),
                            0, axis=1, stride=1, stride_axis=0,
                        )
                        for k in range(kblocks)
                    ]
                    rolled.append(parts)
                for k in range(kblocks):
                    both = [
                        jnp.where(lane < sub, p[k - 1] if k else jnp.zeros_like(p[0]), p[k]) for p in rolled
                    ]
                    ws[c, STRIDE * t : STRIDE * (t + 2), LANES * k : LANES * (k + 1)] = jnp.concatenate(
                        both, axis=0
                    ).astype(jnp.bfloat16)
            numer = jnp.dot(ws[c], zs[c], preferred_element_type=jnp.float32)
            part = numer.reshape(tpls, STRIDE, LANES) * inv[rc][None]
            ratio = part if ratio is None else ratio + part
        for t in range(tpls):
            m = delays[r, t]
            f = m // STRIDE
            e = m - f * STRIDE
            near = pltpu.roll(ratio[t], (LANES - f) % LANES, axis=1)
            far = pltpu.roll(near, LANES - 1, axis=1)
            acc[t] += pltpu.roll(jnp.where(sub < e, far, near), (STRIDE - e) % STRIDE, axis=0)
        return carry

    lax.fori_loop(0, stations, station, 0)

    total = acc[...].reshape(tpls * STRIDE, LANES)
    p1 = total.astype(jnp.bfloat16)
    rest = total - p1.astype(jnp.float32)
    p2 = rest.astype(jnp.bfloat16)
    p3 = (rest - p2.astype(jnp.float32)).astype(jnp.bfloat16)
    spots = iota((LANES, samples), 1) // STRIDE
    spread_out = jnp.where(spots == iota((LANES, samples), 0), 1.0, 0.0).astype(jnp.bfloat16)

    def placed(v):
        return jnp.dot(v, spread_out, preferred_element_type=jnp.float32)

    wide = (placed(p1) + placed(p2) + placed(p3)).reshape(tpls, STRIDE, samples)
    mine = iota((tpls, STRIDE, samples), 2) % STRIDE == iota((tpls, STRIDE, samples), 1)
    out_ref[...] = jnp.sum(jnp.where(mine, wide, 0.0), axis=1)


def correlate(rec, tpl, rowidx, delays, taps):
    stations, tpls = rowidx.shape
    nrc = rec.shape[0] // 2
    samples = rec.shape[1]
    padded = tpl.shape[1]
    channels = nrc // stations
    vm = pl.BlockSpec(memory_space=pltpu.VMEM)
    sm = pl.BlockSpec(memory_space=pltpu.SMEM)
    return pl.pallas_call(
        functools.partial(correlate_kernel, taps),
        out_shape=jax.ShapeDtypeStruct((tpls, samples), jnp.float32),
        in_specs=[sm, sm, vm, vm],
        out_specs=vm,
        scratch_shapes=[
            pltpu.VMEM(tpl.shape, jnp.float32),
            pltpu.VMEM((nrc, STRIDE, LANES), jnp.float32),
            pltpu.VMEM((nrc, STRIDE, LANES), jnp.float32),
            pltpu.VMEM((nrc, STRIDE, LANES), jnp.float32),
            pltpu.VMEM((channels, padded, LANES), jnp.bfloat16),
            pltpu.VMEM((channels, tpls * STRIDE, padded), jnp.bfloat16),
            pltpu.VMEM((tpls, STRIDE, LANES), jnp.float32),
        ],
        compiler_params=pltpu.CompilerParams(vmem_limit_bytes=32 << 20),
    )(rowidx, delays, rec, tpl)


MESH = pl.DeviceIdType.MESH


def exchange_kernel(
    plane, cores, picked, cross_at, own_at, own_here, wave_ref, tpl_ref, rec_ref, all_ref,
    outgoing, arrived, cross, crossed, merged, out_sems, in_sems, pair_sems, halo_sems, line_sems, side_sems
):
    tm, spot = lax.axis_index("tm"), lax.axis_index("tmpl")
    windows = lax.axis_size("tm")
    chips = windows // cores
    chip, core = tm // cores, tm % cores
    half, place = spot // plane, spot % plane
    other_half = 1 - half
    partner = other_half * plane + place
    sibling = chip * cores + (1 - core)
    channels = wave_ref.shape[1]
    slots = outgoing.shape[1] // 2
    table = cross.shape[0] // channels
    taps = tpl_ref.shape[1]

    barrier = pltpu.get_barrier_semaphore()

    def greet(window, group):
        pl.semaphore_signal(barrier, inc=1, device_id=(window, group), device_id_type=MESH)

    def near(step, carry):
        greet(tm, half * plane + (place + step) % plane)
        return carry

    lax.fori_loop(1, plane, near, 0)
    greet(tm, partner)
    greet(sibling, spot)

    @pl.when(chip > 0)
    def _():
        greet(tm - cores, spot)

    @pl.when(chip < chips - 1)
    def _():
        greet(tm + cores, spot)

    @pl.when((core == 0) & (chip > 0))
    def _():
        greet(tm - 1, spot)

    @pl.when((core == 1) & (chip < chips - 1))
    def _():
        greet(tm + 1, spot)

    values = tpl_ref[...].astype(jnp.float32)
    centred = values - jnp.mean(values, axis=-1, keepdims=True)
    factor = lax.rsqrt(jnp.sum(centred * centred, axis=-1, keepdims=True) + 1e-06)
    all_ref[tm] = jnp.zeros(all_ref.shape[1:], all_ref.dtype)
    all_ref[tm, :, :taps] = (centred * factor).astype(all_ref.dtype)

    def gather(step, carry):
        for side in range(2):
            for slot in range(slots):
                outgoing[step, side * slots + slot] = wave_ref[picked[step, side * slots + slot]]
        return carry

    lax.fori_loop(0, plane, gather, 0)
    arrived[place] = outgoing[place]

    after, before = (chip + chips - 1) // chips, (2 * chips - 2 - chip) // chips
    pl.semaphore_wait(barrier, plane + 1 + after * (2 - core) + before * (1 + core))

    def row_copy(step):
        to = (place + step) % plane
        return pltpu.make_async_remote_copy(
            src_ref=outgoing.at[to], dst_ref=arrived.at[place],
            send_sem=out_sems.at[step], recv_sem=in_sems.at[step],
            device_id=(tm, half * plane + to), device_id_type=MESH,
        )

    def line_copy(way, step):
        window = tm - way * cores * step
        lane = (1 - way) // 2
        return pltpu.make_async_remote_copy(
            src_ref=all_ref.at[window], dst_ref=all_ref.at[window],
            send_sem=line_sems.at[lane, 0, step], recv_sem=line_sems.at[lane, 1, step],
            device_id=(tm + way * cores, spot), device_id_type=MESH,
        )

    def side_copy(way, step):
        window = tm - way * cores * step
        lane = (1 - way) // 2
        return pltpu.make_async_remote_copy(
            src_ref=all_ref.at[window], dst_ref=all_ref.at[window],
            send_sem=side_sems.at[lane, 0, step], recv_sem=side_sems.at[lane, 1, step],
            device_id=(sibling, spot), device_id_type=MESH,
        )

    def can_send(way):
        return chip < chips - 1 if way == 1 else chip > 0

    def holds(way, step):
        return chip >= step if way == 1 else chip + step <= chips - 1

    for way in (1, -1):
        @pl.when(can_send(way))
        def _(way=way):
            line_copy(way, 0).start()

    def send_rows(step, carry):
        row_copy(step).start()
        return carry

    lax.fori_loop(1, plane, send_rows, 0)
    side_copy(1, 0).start()

    def relay(step):
        for way in (1, -1):
            @pl.when(holds(way, step))
            def _(way=way):
                line_copy(way, step - 1).wait_recv()
                @pl.when(can_send(way))
                def _():
                    line_copy(way, step).start()
                side_copy(way, step).start()

    relay(1)

    def take_rows(step, carry):
        row_copy(step).wait_recv()
        return carry

    lax.fori_loop(1, plane, take_rows, 0)

    for k in range(table):
        merged[channels * k : channels * (k + 1), :] = arrived[cross_at[k, 0], cross_at[k, 1]].astype(jnp.float32)
    cross[...] = merged[...].astype(cross.dtype)
    pair = pltpu.make_async_remote_copy(
        src_ref=cross, dst_ref=crossed, send_sem=pair_sems.at[0], recv_sem=pair_sems.at[1],
        device_id=(tm, partner), device_id_type=MESH,
    )
    pair.start()

    relay(2)
    relay(3)
    pair.wait_recv()
    far = crossed[...].astype(jnp.float32)
    for k in range(table):
        here = arrived[own_at[k, 0], own_at[k, 1]].astype(jnp.float32)
        merged[channels * k : channels * (k + 1), :] = jnp.where(
            own_here[k] == 1, here, far[channels * k : channels * (k + 1)]
        )
    rec_ref[0] = merged[...].astype(rec_ref.dtype)

    halo = pltpu.make_async_remote_copy(
        src_ref=rec_ref.at[0], dst_ref=rec_ref.at[1], send_sem=halo_sems.at[0], recv_sem=halo_sems.at[1],
        device_id=((tm + windows - 1) % windows, spot), device_id_type=MESH,
    )

    @pl.when(tm > 0)
    def _():
        halo.start()

    for step in range(4, chips):
        relay(step)

    @pl.when(tm == windows - 1)
    def _():
        rec_ref[1] = jnp.zeros(rec_ref.shape[1:], rec_ref.dtype)

    @pl.when(tm < windows - 1)
    def _():
        halo.wait_recv()

    side_copy(1, 0).wait()
    for step in range(1, chips):
        for way in (1, -1):
            @pl.when(holds(way, step))
            def _(way=way, step=step):
                side_copy(way, step).wait()
    for step in range(chips - 1):
        for way in (1, -1):
            @pl.when(holds(way, step) & can_send(way))
            def _(way=way, step=step):
                line_copy(way, step).wait_send()

    def sent_rows(step, carry):
        row_copy(step).wait_send()
        return carry

    lax.fori_loop(1, plane, sent_rows, 0)
    pair.wait_send()

    @pl.when(tm > 0)
    def _():
        halo.wait_send()


def exchange(wave, tpl, picked, cross_at, own_at, own_here, padded):
    windows = lax.axis_size("tm")
    plane = picked.shape[0]
    cores = 2
    channels, samples = wave.shape[1:]
    table = own_here.shape[0]
    nrc = table * channels
    vm = pl.BlockSpec(memory_space=pltpu.VMEM)
    sm = pl.BlockSpec(memory_space=pltpu.SMEM)
    chips = windows // cores
    return pl.pallas_call(
        functools.partial(exchange_kernel, plane, cores),
        out_shape=(
            jax.ShapeDtypeStruct((2, nrc, samples), jnp.bfloat16),
            jax.ShapeDtypeStruct((windows, tpl.shape[0], padded), jnp.bfloat16),
        ),
        in_specs=[sm] * 4 + [vm] * 2,
        out_specs=(vm, vm),
        scratch_shapes=[
            pltpu.VMEM((plane, picked.shape[1], channels, samples), jnp.bfloat16),
            pltpu.VMEM((plane, picked.shape[1], channels, samples), jnp.bfloat16),
            pltpu.VMEM((nrc, samples), jnp.bfloat16),
            pltpu.VMEM((nrc, samples), jnp.bfloat16),
            pltpu.VMEM((nrc, samples), jnp.float32),
            pltpu.SemaphoreType.DMA((plane,)),
            pltpu.SemaphoreType.DMA((plane,)),
            pltpu.SemaphoreType.DMA((2,)),
            pltpu.SemaphoreType.DMA((2,)),
            pltpu.SemaphoreType.DMA((2, 2, chips)),
            pltpu.SemaphoreType.DMA((2, 2, chips)),
        ],
        compiler_params=pltpu.CompilerParams(
            collective_id=0, has_side_effects=True, vmem_limit_bytes=32 << 20
        ),
    )(picked, cross_at, own_at, own_here, wave, tpl)


def routes(group_stations, station_count, plane, capacity):
    spot = lax.axis_index("tmpl")
    half, place = spot // plane, spot % plane
    owners = group_stations // station_count
    locals_ = group_stations % station_count
    table = group_stations.shape[1]
    position = jnp.arange(table, dtype=jnp.int32)
    same = owners[:, :, None] == owners[:, None, :]
    earlier = position[:, None] > position[None, :]
    rank = jnp.sum((same & earlier[None]).astype(jnp.int32), axis=2)
    slots = jnp.arange(capacity, dtype=jnp.int32)
    matched = (owners == spot)[:, :, None] & (rank[:, :, None] == slots)
    picked = jnp.sum(jnp.where(matched, locals_[:, :, None], 0), axis=1)
    picked = picked.reshape(2, plane, capacity).transpose(1, 0, 2).reshape(plane, 2 * capacity)

    def found(group, side):
        mine = lax.dynamic_index_in_dim(owners, group, 0, keepdims=False)
        order = lax.dynamic_index_in_dim(rank, group, 0, keepdims=False)
        return jnp.stack([mine % plane, side * capacity + order], axis=1), mine // plane == half

    cross_at, _ = found((1 - half) * plane + place, 1 - half)
    own_at, own_here = found(spot, half)
    return picked, cross_at, own_at, own_here.astype(jnp.int32)


def per_device(waveforms, templates, group_stations, template_rows, moveouts):
    groups = lax.axis_size("tmpl")
    station_count, channels, samples = waveforms.shape
    table_size = group_stations.shape[1]
    capacity = max(2, 2 * table_size // groups)
    taps = templates.shape[3]
    padded = (taps + LANES - 1) // LANES * LANES
    picked, cross_at, own_at, own_here = routes(group_stations, station_count, groups // 2, capacity)
    rec, tpl = exchange(waveforms, templates[0, 0], picked, cross_at, own_at, own_here, padded)
    rec = rec.reshape(-1, samples)
    tpl = tpl.reshape(-1, padded)
    lists, shifts = template_rows[0], moveouts[0]
    tpls, per_template = lists.shape
    hit = lists[:, :, None] == jnp.arange(table_size, dtype=jnp.int32)
    slot = jnp.sum(jnp.where(hit, jnp.arange(per_template, dtype=jnp.int32)[None, :, None], 0), axis=1)
    delays = jnp.sum(jnp.where(hit, shifts[:, :, None], 0), axis=1)
    base = jnp.arange(tpls, dtype=jnp.int32)[:, None] * (per_template * channels)
    rowidx = base + slot * channels
    return correlate(rec, tpl, rowidx.T, delays.T, taps)[None]


def solution(mesh):
    in_specs = (
        P("tmpl", None, "tm"),
        P("tmpl", "tm", None, None),
        P(),
        P("tmpl", None, None),
        P("tmpl", None, None),
    )
    out_specs = P("tmpl", None, "tm")
    return jax.shard_map(
        per_device, mesh=mesh, in_specs=in_specs, out_specs=out_specs, check_vma=False
    )
```

```python
import functools

import jax
import jax.numpy as jnp
from jax import lax
from jax.experimental import pallas as pl
from jax.experimental.pallas import tpu as pltpu
from jax.sharding import PartitionSpec as P

STRIDE = 8
LANES = 128


def iota(shape, dim):
    return lax.broadcasted_iota(jnp.int32, shape, dim)


def correlate_kernel(
    taps, lists, shifts, near_ref, far_ref, tpl_ref, out_ref, rowidx, delays, tplf, xa, xb, inv, zs, ws, acc
):
    stations, tpls = rowidx.shape
    nrc = xa.shape[0]
    channels = nrc // stations
    samples = near_ref.shape[2]
    frames = samples // STRIDE
    padded = tpl_ref.shape[2]
    kblocks = padded // LANES
    groups = taps // STRIDE + 1
    lane = iota((STRIDE, LANES), 1)
    sub = iota((STRIDE, LANES), 0)

    def use(t, carry):
        for k in range(lists.shape[2]):
            station = lists[0, t, k]
            rowidx[station, t] = t * nrc + k * channels
            delays[station, t] = shifts[0, t, k]
        return carry

    lax.fori_loop(0, tpls, use, 0)
    for t in range(tpls):
        tplf[t * nrc : (t + 1) * nrc, :] = tpl_ref[t].astype(jnp.float32)
    record = (near_ref[...].astype(jnp.float32) + far_ref[...].astype(jnp.float32)).astype(jnp.bfloat16)
    record = record.reshape(2 * nrc, samples)

    gap = iota((samples, LANES), 0) - STRIDE * iota((samples, LANES), 1)
    flat_lane = iota((nrc, LANES), 1)
    for e in range(STRIDE):
        pick = jnp.where(gap == e, 1.0, 0.0).astype(jnp.bfloat16)
        phase = jnp.dot(record, pick, preferred_element_type=jnp.float32)
        later = pltpu.roll(phase[nrc:], frames, axis=1)
        xa[:, e, :] = jnp.where(flat_lane < frames, phase[:nrc], later)
        xb[:, e, :] = later

    ahead = iota((2 * LANES, LANES), 0) - iota((2 * LANES, LANES), 1)
    band = jnp.where((ahead >= 0) & (ahead < taps // STRIDE), 1.0, 0.0).astype(jnp.bfloat16)
    flat = jnp.concatenate([xa[...].reshape(nrc * STRIDE, LANES), xb[...].reshape(nrc * STRIDE, LANES)], axis=1)
    square = flat * flat
    high = square.astype(jnp.bfloat16)
    low = (square - high.astype(jnp.float32)).astype(jnp.bfloat16)

    def banded(v):
        return jnp.dot(v, band, preferred_element_type=jnp.float32)

    def octet(v):
        v = v.reshape(nrc, STRIDE, LANES)
        row = iota((nrc, STRIDE, LANES), 1)
        for k in (1, 2, 4):
            nxt = pltpu.roll(v, LANES - 1, axis=2)
            v = v + pltpu.roll(jnp.where(row < k, nxt, v), STRIDE - k, axis=1)
        return v

    wsum = octet(banded(flat.astype(jnp.bfloat16)))
    wsq = octet(banded(high) + banded(low))
    inv[...] = lax.rsqrt(jnp.maximum(wsq - wsum * wsum / taps, 1.0))

    acc[...] = jnp.zeros_like(acc)
    for i in range(groups, padded // STRIDE, 2):
        for c in range(channels):
            for slot in range(2):
                zs[slot, c, STRIDE * i : STRIDE * (i + 2), :] = jnp.zeros((2 * STRIDE, LANES), jnp.bfloat16)

    def build(r, slot):
        for c in range(channels):
            rc = r * channels + c
            a, b = xa[rc], xb[rc]
            for i in range(0, groups, 2):
                pair = [
                    pltpu.roll(jnp.where(lane < s, b, a), (LANES - s) % LANES, axis=1) for s in (i, i + 1)
                ]
                zs[slot, c, STRIDE * i : STRIDE * (i + 2), :] = jnp.concatenate(pair, axis=0).astype(jnp.bfloat16)
            for t in range(0, tpls, 2):
                rolled = []
                for tt in (t, t + 1):
                    row = tplf[pl.ds(rowidx[r, tt] + c, 1), :]
                    rolled.append([
                        pltpu.roll(
                            jnp.broadcast_to(row[:, LANES * k : LANES * (k + 1)], (STRIDE, LANES)),
                            0, axis=1, stride=1, stride_axis=0,
                        )
                        for k in range(kblocks)
                    ])
                for k in range(kblocks):
                    both = [
                        jnp.where(lane < sub, p[k - 1] if k else jnp.zeros_like(p[0]), p[k]) for p in rolled
                    ]
                    ws[slot, c, STRIDE * t : STRIDE * (t + 2), LANES * k : LANES * (k + 1)] = jnp.concatenate(
                        both, axis=0
                    ).astype(jnp.bfloat16)

    def multiply(slot):
        return [jnp.dot(ws[slot, c], zs[slot, c], preferred_element_type=jnp.float32) for c in range(channels)]

    def settle(r, products):
        ratio = sum(
            products[c].reshape(tpls, STRIDE, LANES) * inv[r * channels + c][None] for c in range(channels)
        )
        for t in range(tpls):
            m = delays[r, t]
            f = m // STRIDE
            e = m - f * STRIDE
            near = pltpu.roll(ratio[t], (LANES - f) % LANES, axis=1)
            far = pltpu.roll(near, LANES - 1, axis=1)
            acc[t] += pltpu.roll(jnp.where(sub < e, far, near), (STRIDE - e) % STRIDE, axis=0)

    build(0, 0)

    def pair_of(p, carry):
        first = 2 * p
        products = multiply(0)
        build(first + 1, 1)
        settle(first, products)
        products = multiply(1)
        build(jnp.minimum(first + 2, stations - 1), 0)
        settle(first + 1, products)
        return carry

    lax.fori_loop(0, stations // 2, pair_of, 0)

    total = acc[...].reshape(tpls * STRIDE, LANES)
    p1 = total.astype(jnp.bfloat16)
    rest = total - p1.astype(jnp.float32)
    p2 = rest.astype(jnp.bfloat16)
    p3 = (rest - p2.astype(jnp.float32)).astype(jnp.bfloat16)
    spots = iota((LANES, samples), 1) // STRIDE
    spread_out = jnp.where(spots == iota((LANES, samples), 0), 1.0, 0.0).astype(jnp.bfloat16)

    def placed(v):
        return jnp.dot(v, spread_out, preferred_element_type=jnp.float32)

    wide = (placed(p1) + placed(p2) + placed(p3)).reshape(tpls, STRIDE, samples)
    mine = iota((tpls, STRIDE, samples), 2) % STRIDE == iota((tpls, STRIDE, samples), 1)
    out_ref[...] = jnp.sum(jnp.where(mine, wide, 0.0), axis=1)


def correlate(near, far, tpl, lists, shifts, taps):
    samples = near.shape[2]
    tpls, nrc, padded = tpl.shape
    stations = lists.shape[2]
    channels = nrc // stations
    vm = pl.BlockSpec(memory_space=pltpu.VMEM)
    sm = pl.BlockSpec(memory_space=pltpu.SMEM)
    return pl.pallas_call(
        functools.partial(correlate_kernel, taps),
        out_shape=jax.ShapeDtypeStruct((tpls, samples), jnp.float32),
        in_specs=[sm, sm, vm, vm, vm],
        out_specs=vm,
        scratch_shapes=[
            pltpu.SMEM((stations, tpls), jnp.int32),
            pltpu.SMEM((stations, tpls), jnp.int32),
            pltpu.VMEM((tpls * nrc, padded), jnp.float32),
            pltpu.VMEM((nrc, STRIDE, LANES), jnp.float32),
            pltpu.VMEM((nrc, STRIDE, LANES), jnp.float32),
            pltpu.VMEM((nrc, STRIDE, LANES), jnp.float32),
            pltpu.VMEM((2, channels, padded, LANES), jnp.bfloat16),
            pltpu.VMEM((2, channels, tpls * STRIDE, padded), jnp.bfloat16),
            pltpu.VMEM((tpls, STRIDE, LANES), jnp.float32),
        ],
        compiler_params=pltpu.CompilerParams(vmem_limit_bytes=32 << 20),
    )(lists, shifts, near, far, tpl)


MESH = pl.DeviceIdType.MESH
REACH = 2
EARLY = (2,)
ORDER = (1, 4, 3, 6, 5, 7)


def exchange_kernel(
    plane, cores, slots, table_hbm, wave_hbm, tpl_hbm, near_ref, far_ref, all_ref,
    table, wave, raw, picked, chosen, outgoing, arrived, cross,
    load_sems, out_sems, in_sems, pair_sems, halo_sems, line_sends, line_recvs, side_sends, side_recvs
):
    tm, spot = lax.axis_index("tm"), lax.axis_index("tmpl")
    windows = lax.axis_size("tm")
    chips = windows // cores
    chip, core = tm // cores, tm % cores
    half, place = spot // plane, spot % plane
    partner = (1 - half) * plane + place
    sibling = chip * cores + (1 - core)
    channels, stored, samples = wave.shape
    stations, groups = table.shape
    unit = arrived.shape[1]
    taps = raw.shape[1]

    loads = [
        pltpu.make_async_copy(src, dst, load_sems.at[n])
        for n, (src, dst) in enumerate([(table_hbm, table), (wave_hbm, wave), (tpl_hbm, raw)])
    ]
    for load in loads:
        load.start()

    barrier = pltpu.get_barrier_semaphore()

    def greet(window, group):
        pl.semaphore_signal(barrier, inc=1, device_id=(window, group), device_id_type=MESH)

    def room(way):
        return chips - 1 - chip if way == 1 else chip

    def greet_plane(step, carry):
        greet(tm, half * plane + (place + step) % plane)
        return carry

    greet(tm, partner)
    lax.fori_loop(1, plane, greet_plane, 0)
    for step in range(1, REACH + 1):
        for way in (1, -1):
            @pl.when(room(way) >= step)
            def _(way=way, step=step):
                greet(tm + way * cores * step, spot)
    greet(sibling, spot)

    @pl.when((core == 0) & (chip > 0))
    def _():
        greet(tm - 1, spot)

    @pl.when((core == 1) & (chip < chips - 1))
    def _():
        greet(tm + 1, spot)

    loads[0].wait()
    base = spot * stored

    def scan(group, carry):
        count = 0
        found = [0] * slots
        for k in range(stations):
            gap = table[k, group] - base
            hit = (gap >= 0) & (gap < stored)
            found = [jnp.where(hit & (count == n), gap, found[n]) for n in range(slots)]
            count = count + jnp.where(hit, 1, 0)
        for n in range(slots):
            picked[group % plane, (group // plane) * slots + n] = found[n]
        return carry

    lax.fori_loop(0, groups, scan, 0)
    loads[1].wait()

    row = iota((unit, channels * stored), 0)
    column = iota((unit, channels * stored), 1)

    def choose(step, carry):
        want = jnp.where(row < 2 * slots * channels, row % channels * stored, -stored)
        for n in range(2 * slots):
            want = want + jnp.where(row // channels == n, picked[step, n], 0)
        chosen[pl.ds(pl.multiple_of(step * unit, unit), unit), :] = jnp.where(column == want, 1.0, 0.0).astype(chosen.dtype)
        return carry

    lax.fori_loop(0, plane, choose, 0)
    outgoing[...] = jnp.dot(
        chosen[...], wave[...].reshape(channels * stored, samples), preferred_element_type=jnp.float32
    ).astype(outgoing.dtype).reshape(outgoing.shape)
    arrived[place] = outgoing[place]

    spots = iota((stations * channels, plane * unit), 0)
    order = iota((stations * channels, plane * unit), 1)

    def collect(group, side):
        want = spots % channels
        owners = []
        for k in range(stations):
            station = table[k, group]
            owner = station // stored
            rank = 0
            for earlier in owners:
                rank = rank + jnp.where(earlier == owner, 1, 0)
            owners.append(owner)
            place_of = owner % plane * unit + (side * slots + rank) * channels
            place_of = jnp.where(owner // plane == half, place_of, -channels)
            want = want + jnp.where(spots // channels == k, place_of, 0)
        return jnp.where(order == want, 1.0, 0.0).astype(arrived.dtype)

    across = collect(partner, 1 - half)
    local = collect(spot, half)

    loads[2].wait()
    values = raw[...].astype(jnp.float32)
    centred = values - jnp.mean(values, axis=-1, keepdims=True)
    factor = lax.rsqrt(jnp.sum(centred * centred, axis=-1, keepdims=True) + 1e-06)
    all_ref[tm] = jnp.zeros(all_ref.shape[1:], all_ref.dtype)
    all_ref[tm, :, :taps] = (centred * factor).astype(all_ref.dtype)

    peers = plane + 1
    for step in range(1, REACH + 1):
        for way in (1, -1):
            peers = peers + (room(way) + chips - step) // chips
    peers = peers + (1 - core) * ((chip + chips - 1) // chips) + core * ((2 * chips - 2 - chip) // chips)
    pl.semaphore_wait(barrier, peers)

    def row_copy(step):
        to = (place + step) % plane
        return pltpu.make_async_remote_copy(
            src_ref=outgoing.at[to], dst_ref=arrived.at[place],
            send_sem=out_sems.at[step], recv_sem=in_sems.at[step],
            device_id=(tm, half * plane + to), device_id_type=MESH,
        )

    def line_copy(way, come, go):
        window = tm - way * cores * come
        lane = (1 - way) // 2
        return pltpu.make_async_remote_copy(
            src_ref=all_ref.at[window], dst_ref=all_ref.at[window],
            send_sem=line_sends.at[lane, come + go], recv_sem=line_recvs.at[lane, come + go],
            device_id=(tm + way * cores * go, spot), device_id_type=MESH,
        )

    def side_copy(way, come):
        window = tm - way * cores * come
        lane = (1 - way) // 2
        return pltpu.make_async_remote_copy(
            src_ref=all_ref.at[window], dst_ref=all_ref.at[window],
            send_sem=side_sends.at[lane, come], recv_sem=side_recvs.at[lane, come],
            device_id=(sibling, spot), device_id_type=MESH,
        )

    def send_rows(step, carry):
        row_copy(step).start()
        return carry

    def take_rows(step, carry):
        row_copy(step).wait_recv()
        return carry

    def sent_rows(step, carry):
        row_copy(step).wait_send()
        return carry

    lax.fori_loop(1, plane, send_rows, 0)
    for go in range(REACH, 0, -1):
        for way in (1, -1):
            @pl.when(room(way) >= go)
            def _(way=way, go=go):
                line_copy(way, 0, go).start()
    side_copy(1, 0).start()

    def receive(come):
        for way in (1, -1):
            @pl.when(room(-way) >= come)
            def _(way=way):
                line_copy(way, come, 0).wait_recv()
                if come % REACH == 0:
                    for go in range(min(REACH, chips - 1 - come), 0, -1):
                        @pl.when(room(way) >= go)
                        def _(go=go):
                            line_copy(way, come, go).start()
                side_copy(way, come).start()

    for come in EARLY:
        receive(come)
    lax.fori_loop(1, plane, take_rows, 0)

    def pull(hot):
        rows = arrived[...].reshape(plane * unit, samples)
        return jnp.dot(hot, rows, preferred_element_type=jnp.float32).astype(arrived.dtype)

    cross[...] = pull(across)
    pair = pltpu.make_async_remote_copy(
        src_ref=cross, dst_ref=far_ref.at[0], send_sem=pair_sems.at[0], recv_sem=pair_sems.at[1],
        device_id=(tm, partner), device_id_type=MESH,
    )
    pair.start()
    near_ref[0] = pull(local)

    def halo(n):
        ref = (near_ref, far_ref)[n]
        return pltpu.make_async_remote_copy(
            src_ref=ref.at[0], dst_ref=ref.at[1], send_sem=halo_sems.at[n, 0], recv_sem=halo_sems.at[n, 1],
            device_id=((tm + windows - 1) % windows, spot), device_id_type=MESH,
        )

    @pl.when(tm > 0)
    def _():
        halo(0).start()

    @pl.when(tm == windows - 1)
    def _():
        near_ref[1] = jnp.zeros(near_ref.shape[1:], near_ref.dtype)
        far_ref[1] = jnp.zeros(far_ref.shape[1:], far_ref.dtype)

    for come in ORDER:
        receive(come)

    pair.wait_recv()

    @pl.when(tm > 0)
    def _():
        halo(1).start()

    side_copy(1, 0).wait()
    for come in range(1, chips):
        for way in (1, -1):
            @pl.when(room(-way) >= come)
            def _(way=way, come=come):
                side_copy(way, come).wait()
    for come in range(0, chips, REACH):
        for go in range(1, min(REACH, chips - 1 - come) + 1):
            for way in (1, -1):
                @pl.when((room(-way) >= come) & (room(way) >= go))
                def _(way=way, come=come, go=go):
                    line_copy(way, come, go).wait_send()
    lax.fori_loop(1, plane, sent_rows, 0)
    pair.wait_send()

    @pl.when(tm < windows - 1)
    def _():
        halo(0).wait_recv()
        halo(1).wait_recv()

    @pl.when(tm > 0)
    def _():
        halo(0).wait_send()
        halo(1).wait_send()


def exchange(table, wave, tpl, slots, padded):
    windows = lax.axis_size("tm")
    cores = 2
    stations, groups = table.shape
    plane = groups // 2
    channels, stored, samples = wave.shape
    unit = -(-2 * slots * channels // 8) * 8
    nrc = stations * channels
    vm = pl.BlockSpec(memory_space=pltpu.VMEM)
    hbm = pl.BlockSpec(memory_space=pltpu.HBM)
    chips = windows // cores
    record = jax.ShapeDtypeStruct((2, nrc, samples), jnp.bfloat16)
    return pl.pallas_call(
        functools.partial(exchange_kernel, plane, cores, slots),
        out_shape=(record, record, jax.ShapeDtypeStruct((windows, tpl.shape[0], padded), jnp.bfloat16)),
        in_specs=[hbm] * 3,
        out_specs=(vm, vm, vm),
        scratch_shapes=[
            pltpu.SMEM(table.shape, jnp.int32),
            pltpu.VMEM(wave.shape, wave.dtype),
            pltpu.VMEM(tpl.shape, tpl.dtype),
            pltpu.SMEM((plane, 2 * slots), jnp.int32),
            pltpu.VMEM((plane * unit, channels * stored), jnp.bfloat16),
            pltpu.VMEM((plane, unit, samples), jnp.bfloat16),
            pltpu.VMEM((plane, unit, samples), jnp.bfloat16),
            pltpu.VMEM((nrc, samples), jnp.bfloat16),
            pltpu.SemaphoreType.DMA((3,)),
            pltpu.SemaphoreType.DMA((plane,)),
            pltpu.SemaphoreType.DMA((plane,)),
            pltpu.SemaphoreType.DMA((2,)),
            pltpu.SemaphoreType.DMA((2, 2)),
            pltpu.SemaphoreType.DMA((2, chips)),
            pltpu.SemaphoreType.DMA((2, chips)),
            pltpu.SemaphoreType.DMA((2, chips)),
            pltpu.SemaphoreType.DMA((2, chips)),
        ],
        compiler_params=pltpu.CompilerParams(
            collective_id=0, has_side_effects=True, vmem_limit_bytes=32 << 20
        ),
    )(table, wave, tpl)


def per_device(waveforms, templates, group_stations, template_rows, moveouts):
    table_size = group_stations.shape[1]
    slots = max(2, 2 * table_size // lax.axis_size("tmpl"))
    taps = templates.shape[3]
    padded = (taps + LANES - 1) // LANES * LANES
    near, far, tpl = exchange(
        group_stations.T, waveforms.transpose(1, 0, 2), templates[0, 0], slots, padded
    )
    return correlate(near, far, tpl, template_rows, moveouts, taps)[None]


def solution(mesh):
    in_specs = (
        P("tmpl", None, "tm"),
        P("tmpl", "tm", None, None),
        P(),
        P("tmpl", None, None),
        P("tmpl", None, None),
    )
    out_specs = P("tmpl", None, "tm")
    return jax.shard_map(
        per_device, mesh=mesh, in_specs=in_specs, out_specs=out_specs, check_vma=False
    )
```

```python
import functools

import jax
import jax.numpy as jnp
from jax import lax
from jax.experimental import pallas as pl
from jax.experimental.pallas import tpu as pltpu
from jax.sharding import PartitionSpec as P

STRIDE = 8
LANES = 128

MESH = pl.DeviceIdType.MESH
REACH = 2
EARLY = (2,)
ORDER = (1, 4, 3, 6, 5, 7)
FORWARD = 6


def iota(shape, dim):
    return lax.broadcasted_iota(jnp.int32, shape, dim)


def matched_filter_kernel(
    plane, cores, slots, taps, table_hbm, lists_hbm, shifts_hbm, wave_hbm, tpl_hbm, out_ref,
    table, lists, shifts, wave, raw, picked, chosen, outgoing, arrived, cross, near_ref, far_ref, all_ref,
    use_pair, rowidx, delays, picks, band, plain, shifted, xa, xb, inv, xa16, xb16, zs, acc,
    load_sems, out_sems, in_sems, pair_sems, halo_sems, line_sends, line_recvs, side_sends, side_recvs
):
    tm, spot = lax.axis_index("tm"), lax.axis_index("tmpl")
    windows = lax.axis_size("tm")
    chips = windows // cores
    chip, core = tm // cores, tm % cores
    half, place = spot // plane, spot % plane
    partner = (1 - half) * plane + place
    sibling = chip * cores + (1 - core)
    channels, stored, samples = wave.shape
    stations, groups = table.shape
    unit = arrived.shape[1]

    loads = [
        pltpu.make_async_copy(src, dst, load_sems.at[n])
        for n, (src, dst) in enumerate([(table_hbm, table), (wave_hbm, wave), (tpl_hbm, raw), (lists_hbm, lists), (shifts_hbm, shifts)])
    ]
    for load in loads:
        load.start()

    barrier = pltpu.get_barrier_semaphore()

    def greet(window, group):
        pl.semaphore_signal(barrier, inc=1, device_id=(window, group), device_id_type=MESH)

    def room(way):
        return chips - 1 - chip if way == 1 else chip

    def greet_plane(step, carry):
        greet(tm, half * plane + (place + step) % plane)
        return carry

    greet(tm, partner)
    lax.fori_loop(1, plane, greet_plane, 0)
    for step in range(1, REACH + 1):
        for way in (1, -1):
            @pl.when(room(way) >= step)
            def _(way=way, step=step):
                greet(tm + way * cores * step, spot)
    greet(sibling, spot)

    @pl.when((core == 0) & (chip > 0))
    def _():
        greet(tm - 1, spot)

    @pl.when((core == 1) & (chip < chips - 1))
    def _():
        greet(tm + 1, spot)

    loads[0].wait()
    base = spot * stored

    def scan(group, carry):
        count = 0
        found = [0] * slots
        for k in range(stations):
            gap = table[k, group] - base
            hit = (gap >= 0) & (gap < stored)
            found = [jnp.where(hit & (count == n), gap, found[n]) for n in range(slots)]
            count = count + jnp.where(hit, 1, 0)
        for n in range(slots):
            picked[group % plane, (group // plane) * slots + n] = found[n]
        return carry

    lax.fori_loop(0, groups, scan, 0)
    loads[1].wait()

    row = iota((unit, channels * stored), 0)
    column = iota((unit, channels * stored), 1)

    def choose(step, carry):
        want = jnp.where(row < 2 * slots * channels, row % channels * stored, -stored)
        for n in range(2 * slots):
            want = want + jnp.where(row // channels == n, picked[step, n], 0)
        chosen[pl.ds(pl.multiple_of(step * unit, unit), unit), :] = jnp.where(column == want, 1.0, 0.0).astype(chosen.dtype)
        return carry

    lax.fori_loop(0, plane, choose, 0)
    outgoing[...] = jnp.dot(
        chosen[...], wave[...].reshape(channels * stored, samples), preferred_element_type=jnp.float32
    ).astype(outgoing.dtype).reshape(outgoing.shape)
    arrived[place] = outgoing[place]

    spots = iota((stations * channels, plane * unit), 0)
    order = iota((stations * channels, plane * unit), 1)

    def collect(group, side):
        want = spots % channels
        owners = []
        for k in range(stations):
            station = table[k, group]
            owner = station // stored
            rank = 0
            for earlier in owners:
                rank = rank + jnp.where(earlier == owner, 1, 0)
            owners.append(owner)
            place_of = owner % plane * unit + (side * slots + rank) * channels
            place_of = jnp.where(owner // plane == half, place_of, -channels)
            want = want + jnp.where(spots // channels == k, place_of, 0)
        return jnp.where(order == want, 1.0, 0.0).astype(arrived.dtype)

    across = collect(partner, 1 - half)
    local = collect(spot, half)

    loads[2].wait()
    values = raw[...].astype(jnp.float32)
    centred = values - jnp.mean(values, axis=-1, keepdims=True)
    factor = lax.rsqrt(jnp.sum(centred * centred, axis=-1, keepdims=True) + 1e-06)
    all_ref[tm] = jnp.zeros(all_ref.shape[1:], all_ref.dtype)
    all_ref[tm, :, :taps] = (centred * factor).astype(all_ref.dtype)

    peers = plane + 1
    for step in range(1, REACH + 1):
        for way in (1, -1):
            peers = peers + (room(way) + chips - step) // chips
    peers = peers + (1 - core) * ((chip + chips - 1) // chips) + core * ((2 * chips - 2 - chip) // chips)
    pl.semaphore_wait(barrier, peers)

    def row_copy(step):
        to = (place + step) % plane
        return pltpu.make_async_remote_copy(
            src_ref=outgoing.at[to], dst_ref=arrived.at[place],
            send_sem=out_sems.at[step], recv_sem=in_sems.at[step],
            device_id=(tm, half * plane + to), device_id_type=MESH,
        )

    def line_copy(way, come, go):
        window = tm - way * cores * come
        lane = (1 - way) // 2
        return pltpu.make_async_remote_copy(
            src_ref=all_ref.at[window], dst_ref=all_ref.at[window],
            send_sem=line_sends.at[lane, come + go], recv_sem=line_recvs.at[lane, come + go],
            device_id=(tm + way * cores * go, spot), device_id_type=MESH,
        )

    def side_copy(way, come):
        window = tm - way * cores * come
        lane = (1 - way) // 2
        return pltpu.make_async_remote_copy(
            src_ref=all_ref.at[window], dst_ref=all_ref.at[window],
            send_sem=side_sends.at[lane, come], recv_sem=side_recvs.at[lane, come],
            device_id=(sibling, spot), device_id_type=MESH,
        )

    def send_rows(step, carry):
        row_copy(step).start()
        return carry

    def take_rows(step, carry):
        row_copy(step).wait_recv()
        return carry

    def sent_rows(step, carry):
        row_copy(step).wait_send()
        return carry

    lax.fori_loop(1, plane, send_rows, 0)
    for go in range(REACH, 0, -1):
        for way in (1, -1):
            @pl.when(room(way) >= go)
            def _(way=way, go=go):
                line_copy(way, 0, go).start()
    side_copy(1, 0).start()

    def receive(come):
        for way in (1, -1):
            @pl.when(room(-way) >= come)
            def _(way=way):
                line_copy(way, come, 0).wait_recv()
                if come % REACH == 0:
                    for go in range(min(REACH, chips - 1 - come), 0, -1):
                        @pl.when(room(way) >= go)
                        def _(go=go):
                            line_copy(way, come, go).start()
                side_copy(way, come).start()

    for come in EARLY:
        receive(come)

    tpls, nrc = lists.shape[0], stations * channels
    frames = samples // STRIDE
    padded = all_ref.shape[2]
    steps = taps // STRIDE + 1
    gap = iota((samples, LANES), 0) - STRIDE * iota((samples, LANES), 1)
    for e in range(STRIDE):
        picks[e] = jnp.where(gap == e, 1.0, 0.0).astype(picks.dtype)
    ahead = iota((2 * LANES, LANES), 0) - iota((2 * LANES, LANES), 1)
    band[...] = jnp.where((ahead >= 0) & (ahead < taps // STRIDE), 1.0, 0.0).astype(band.dtype)
    for slot in range(2):
        for c in range(channels):
            zs[slot, c, STRIDE * steps :, :] = jnp.zeros((padded - STRIDE * steps, LANES), zs.dtype)
    acc[...] = jnp.zeros_like(acc)

    loads[3].wait()
    loads[4].wait()
    who, lag = lists[...], shifts[...]
    entry = iota(who.shape, 1)
    first, late = jnp.zeros_like(who), jnp.zeros_like(who)
    for r in range(stations):
        hit = who == r
        first = jnp.where(entry == r, jnp.max(jnp.where(hit, entry, 0), axis=1, keepdims=True), first)
        late = jnp.where(entry == r, jnp.max(jnp.where(hit, lag, 0), axis=1, keepdims=True), late)
    use_pair[0] = first * channels + iota(who.shape, 0) * nrc
    use_pair[1] = late
    uses = [
        pltpu.make_async_copy(use_pair.at[n], dst, load_sems.at[5 + n]) for n, dst in enumerate((rowidx, delays))
    ]
    for use in uses:
        use.start()

    lax.fori_loop(1, plane, take_rows, 0)

    def pull(hot):
        rows = arrived[...].reshape(plane * unit, samples)
        return jnp.dot(hot, rows, preferred_element_type=jnp.float32).astype(arrived.dtype)

    cross[...] = pull(across)
    pair = pltpu.make_async_remote_copy(
        src_ref=cross, dst_ref=far_ref.at[0], send_sem=pair_sems.at[0], recv_sem=pair_sems.at[1],
        device_id=(tm, partner), device_id_type=MESH,
    )
    pair.start()
    near_ref[0] = pull(local)

    def halo(n):
        ref = (near_ref, far_ref)[n]
        return pltpu.make_async_remote_copy(
            src_ref=ref.at[0], dst_ref=ref.at[1], send_sem=halo_sems.at[n, 0], recv_sem=halo_sems.at[n, 1],
            device_id=((tm + windows - 1) % windows, spot), device_id_type=MESH,
        )

    @pl.when(tm > 0)
    def _():
        halo(0).start()

    @pl.when(tm == windows - 1)
    def _():
        near_ref[1] = jnp.zeros(near_ref.shape[1:], near_ref.dtype)
        far_ref[1] = jnp.zeros(far_ref.shape[1:], far_ref.dtype)

    lane = iota((STRIDE, LANES), 1)
    sub = iota((STRIDE, LANES), 0)

    def spread_taps(window):
        plain[...] = all_ref[window].astype(jnp.float32)

        def eight(part, carry):
            start = pl.multiple_of(part * STRIDE, STRIDE)
            for n in range(STRIDE):
                row = plain[pl.ds(start + n, 1), :]
                before = jnp.zeros((STRIDE, LANES), jnp.float32)
                for b in range(padded // LANES):
                    here = pltpu.roll(
                        jnp.broadcast_to(row[:, LANES * b : LANES * (b + 1)], (STRIDE, LANES)),
                        0, axis=1, stride=1, stride_axis=0,
                    )
                    shifted[window * nrc + start + n, :, LANES * b : LANES * (b + 1)] = jnp.where(
                        lane < sub, before, here
                    ).astype(shifted.dtype)
                    before = here
            return carry

        lax.fori_loop(0, nrc // STRIDE, eight, 0)

    def take_line(come):
        for way in (1, -1):
            @pl.when(room(-way) >= come)
            def _(way=way):
                spread_taps(tm - way * cores * come)

    def take_side(come):
        for way in (1, -1):
            @pl.when(room(-way) >= come)
            def _(way=way):
                side_copy(way, come).wait()
                spread_taps(sibling - way * cores * come)

    spread_taps(tm)
    take_line(REACH)
    side_copy(1, 0).wait()
    spread_taps(sibling)
    last = REACH
    for come in ORDER:
        receive(come)
        if come == FORWARD:
            pair.wait_recv()

            @pl.when(tm > 0)
            def _():
                halo(1).start()

        take_line(come)
        take_side(last)
        last = come
    own = near_ref[0].astype(jnp.float32) + far_ref[0].astype(jnp.float32)
    own = own.astype(jnp.bfloat16)
    for e in range(STRIDE):
        xa[:, e, :] = jnp.dot(own, picks[e], preferred_element_type=jnp.float32)
    take_side(last)

    for come in range(0, chips, REACH):
        for go in range(1, min(REACH, chips - 1 - come) + 1):
            for way in (1, -1):
                @pl.when((room(-way) >= come) & (room(way) >= go))
                def _(way=way, come=come, go=go):
                    line_copy(way, come, go).wait_send()
    lax.fori_loop(1, plane, sent_rows, 0)
    pair.wait_send()

    @pl.when(tm < windows - 1)
    def _():
        halo(0).wait_recv()
        halo(1).wait_recv()

    @pl.when(tm > 0)
    def _():
        halo(0).wait_send()
        halo(1).wait_send()

    for use in uses:
        use.wait()
    later_rows = near_ref[1].astype(jnp.float32) + far_ref[1].astype(jnp.float32)
    later_rows = later_rows.astype(jnp.bfloat16)
    flat_lane = iota((nrc, LANES), 1)
    for e in range(STRIDE):
        phase = jnp.dot(later_rows, picks[e], preferred_element_type=jnp.float32)
        later = pltpu.roll(phase, frames, axis=1)
        xa[:, e, :] = jnp.where(flat_lane < frames, xa[:, e, :], later)
        xb[:, e, :] = later

    flat = jnp.concatenate([xa[...].reshape(nrc * STRIDE, LANES), xb[...].reshape(nrc * STRIDE, LANES)], axis=1)
    square = flat * flat
    high = square.astype(jnp.bfloat16)
    low = (square - high.astype(jnp.float32)).astype(jnp.bfloat16)

    def banded(v):
        return jnp.dot(v, band[...], preferred_element_type=jnp.float32)

    def octet(v):
        v = v.reshape(nrc, STRIDE, LANES)
        row = iota((nrc, STRIDE, LANES), 1)
        for k in (1, 2, 4):
            nxt = pltpu.roll(v, LANES - 1, axis=2)
            v = v + pltpu.roll(jnp.where(row < k, nxt, v), STRIDE - k, axis=1)
        return v

    wsum = octet(banded(flat.astype(jnp.bfloat16)))
    wsq = octet(banded(high) + banded(low))
    inv[...] = lax.rsqrt(jnp.maximum(wsq - wsum * wsum / taps, 1.0))

    lane16 = iota((2 * STRIDE, LANES), 1)
    wide = iota((nrc, STRIDE, LANES), 2)
    next_b = pltpu.roll(xb[...], LANES - 1, axis=2)
    next_a = jnp.where(wide < LANES - 1, pltpu.roll(xa[...], LANES - 1, axis=2), next_b)
    xa16[...] = jnp.concatenate([xa[...], next_a], axis=1).astype(jnp.bfloat16)
    xb16[...] = jnp.concatenate([xb[...], next_b], axis=1).astype(jnp.bfloat16)
    def build(r, slot):
        for c in range(channels):
            rc = r * channels + c
            a, b = xa16[rc], xb16[rc]
            for i in range(0, steps, 2):
                mixed = jnp.where(lane16 < i, b, a) if i else a
                zs[slot, c, STRIDE * i : STRIDE * (i + 2), :] = pltpu.roll(mixed, LANES - i, axis=1) if i else a

    def multiply(r, slot):
        products = []
        for c in range(channels):
            left = jnp.concatenate([shifted[rowidx[t, r] + c] for t in range(tpls)], axis=0)
            products.append(jnp.dot(left, zs[slot, c], preferred_element_type=jnp.float32))
        return products

    def settle(r, products):
        ratio = sum(
            products[c].reshape(tpls, STRIDE, LANES) * inv[r * channels + c][None] for c in range(channels)
        )
        for t in range(tpls):
            m = delays[t, r]
            f = m // STRIDE
            e = m - f * STRIDE
            near = pltpu.roll(ratio[t], (LANES - f) % LANES, axis=1)
            far = pltpu.roll(near, LANES - 1, axis=1)
            acc[t] += pltpu.roll(jnp.where(sub < e, far, near), (STRIDE - e) % STRIDE, axis=0)

    build(0, 0)

    def pair_of(p, carry):
        first = 2 * p
        products = multiply(first, 0)
        build(first + 1, 1)
        settle(first, products)
        products = multiply(first + 1, 1)
        build(jnp.minimum(first + 2, stations - 1), 0)
        settle(first + 1, products)
        return carry

    lax.fori_loop(0, stations // 2, pair_of, 0)

    total = acc[...].reshape(tpls * STRIDE, LANES)
    p1 = total.astype(jnp.bfloat16)
    rest = total - p1.astype(jnp.float32)
    p2 = rest.astype(jnp.bfloat16)
    p3 = (rest - p2.astype(jnp.float32)).astype(jnp.bfloat16)
    spots = iota((LANES, samples), 1) // STRIDE
    spread_out = jnp.where(spots == iota((LANES, samples), 0), 1.0, 0.0).astype(jnp.bfloat16)

    def placed(v):
        return jnp.dot(v, spread_out, preferred_element_type=jnp.float32)

    wide = (placed(p1) + placed(p2) + placed(p3)).reshape(tpls, STRIDE, samples)
    mine = iota((tpls, STRIDE, samples), 2) % STRIDE == iota((tpls, STRIDE, samples), 1)
    out_ref[...] = jnp.sum(jnp.where(mine, wide, 0.0), axis=1)


def matched_filter(table, lists, shifts, wave, tpl, slots, padded):
    windows = lax.axis_size("tm")
    cores = 2
    stations, groups = table.shape
    plane = groups // 2
    channels, stored, samples = wave.shape
    unit = -(-2 * slots * channels // 8) * 8
    nrc = stations * channels
    tpls = lists.shape[0]
    chips = windows // cores
    operands = (table, lists, shifts, wave, tpl)
    return pl.pallas_call(
        functools.partial(matched_filter_kernel, plane, cores, slots, tpl.shape[1]),
        out_shape=jax.ShapeDtypeStruct((tpls, samples), jnp.float32),
        in_specs=[pl.BlockSpec(memory_space=pltpu.HBM)] * len(operands),
        out_specs=pl.BlockSpec(memory_space=pltpu.VMEM),
        scratch_shapes=[
            pltpu.SMEM(table.shape, jnp.int32),
            pltpu.VMEM(lists.shape, jnp.int32),
            pltpu.VMEM(shifts.shape, jnp.int32),
            pltpu.VMEM(wave.shape, wave.dtype),
            pltpu.VMEM(tpl.shape, tpl.dtype),
            pltpu.SMEM((plane, 2 * slots), jnp.int32),
            pltpu.VMEM((plane * unit, channels * stored), jnp.bfloat16),
            pltpu.VMEM((plane, unit, samples), jnp.bfloat16),
            pltpu.VMEM((plane, unit, samples), jnp.bfloat16),
            pltpu.VMEM((nrc, samples), jnp.bfloat16),
            pltpu.VMEM((2, nrc, samples), jnp.bfloat16),
            pltpu.VMEM((2, nrc, samples), jnp.bfloat16),
            pltpu.VMEM((windows, tpl.shape[0], padded), jnp.bfloat16),
            pltpu.VMEM((2, *lists.shape), jnp.int32),
            pltpu.SMEM(lists.shape, jnp.int32),
            pltpu.SMEM(lists.shape, jnp.int32),
            pltpu.VMEM((STRIDE, samples, LANES), jnp.bfloat16),
            pltpu.VMEM((2 * LANES, LANES), jnp.bfloat16),
            pltpu.VMEM((nrc, padded), jnp.float32),
            pltpu.VMEM((tpls * nrc, STRIDE, padded), jnp.bfloat16),
            pltpu.VMEM((nrc, STRIDE, LANES), jnp.float32),
            pltpu.VMEM((nrc, STRIDE, LANES), jnp.float32),
            pltpu.VMEM((nrc, STRIDE, LANES), jnp.float32),
            pltpu.VMEM((nrc, 2 * STRIDE, LANES), jnp.bfloat16),
            pltpu.VMEM((nrc, 2 * STRIDE, LANES), jnp.bfloat16),
            pltpu.VMEM((2, channels, padded, LANES), jnp.bfloat16),
            pltpu.VMEM((tpls, STRIDE, LANES), jnp.float32),
            pltpu.SemaphoreType.DMA((7,)),
            pltpu.SemaphoreType.DMA((plane,)),
            pltpu.SemaphoreType.DMA((plane,)),
            pltpu.SemaphoreType.DMA((2,)),
            pltpu.SemaphoreType.DMA((2, 2)),
            pltpu.SemaphoreType.DMA((2, chips)),
            pltpu.SemaphoreType.DMA((2, chips)),
            pltpu.SemaphoreType.DMA((2, chips)),
            pltpu.SemaphoreType.DMA((2, chips)),
        ],
        compiler_params=pltpu.CompilerParams(
            collective_id=0, has_side_effects=True, vmem_limit_bytes=40 << 20
        ),
    )(*(pltpu.with_memory_space_constraint(v, pltpu.HBM) for v in operands))


def per_device(waveforms, templates, group_stations, template_rows, moveouts):
    slots = max(2, 2 * group_stations.shape[1] // lax.axis_size("tmpl"))
    padded = (templates.shape[3] + LANES - 1) // LANES * LANES
    return matched_filter(
        group_stations.T, template_rows[0], moveouts[0], waveforms.transpose(1, 0, 2), templates[0, 0], slots, padded
    )[None]


def solution(mesh):
    in_specs = (
        P("tmpl", None, "tm"),
        P("tmpl", "tm", None, None),
        P(),
        P("tmpl", None, None),
        P("tmpl", None, None),
    )
    out_specs = P("tmpl", None, "tm")
    return jax.shard_map(
        per_device, mesh=mesh, in_specs=in_specs, out_specs=out_specs, check_vma=False
    )
```

```python
import functools

import jax
import jax.numpy as jnp
from jax import lax
from jax.experimental import pallas as pl
from jax.experimental.pallas import tpu as pltpu
from jax.sharding import PartitionSpec as P

STRIDE = 8
LANES = 128

MESH = pl.DeviceIdType.MESH
HOPS = {0: 2, 2: 3, 5: 2}
REACH = max(HOPS.values())
EARLY = (2,)
ORDER = (1, 5, 4, 3, 6, 7)
FORWARD = 3


def iota(shape, dim):
    return lax.broadcasted_iota(jnp.int32, shape, dim)


def matched_filter_kernel(
    plane, cores, slots, taps, table_hbm, lists_hbm, shifts_hbm, wave_hbm, tpl_hbm, out_ref,
    table, lists, shifts, wave, raw, picked, chosen, outgoing, arrived, cross, near_ref, far_ref, all_ref,
    use_pair, rowidx, delays, picks, band, plain, shifted, xa, xb, inv, xa16, xb16, zs, acc,
    load_sems, out_sems, in_sems, pair_sems, halo_sems, line_sends, line_recvs, side_sends, side_recvs
):
    tm, spot = lax.axis_index("tm"), lax.axis_index("tmpl")
    windows = lax.axis_size("tm")
    chips = windows // cores
    chip, core = tm // cores, tm % cores
    half, place = spot // plane, spot % plane
    partner = (1 - half) * plane + place
    sibling = chip * cores + (1 - core)
    channels, stored, samples = wave.shape
    stations, groups = table.shape
    unit = arrived.shape[1]

    loads = [
        pltpu.make_async_copy(src, dst, load_sems.at[n])
        for n, (src, dst) in enumerate([(table_hbm, table), (wave_hbm, wave), (tpl_hbm, raw), (lists_hbm, lists), (shifts_hbm, shifts)])
    ]
    barrier = pltpu.get_barrier_semaphore()

    def greet(window, group):
        pl.semaphore_signal(barrier, inc=1, device_id=(window, group), device_id_type=MESH)

    def room(way):
        return chips - 1 - chip if way == 1 else chip

    def start_loads():
        for load in loads:
            load.start()

    def greet_plane(step, carry):
        greet(tm, half * plane + (place + step) % plane)
        return carry

    greet(tm, partner)
    lax.fori_loop(1, plane, greet_plane, 0)
    start_loads()
    for step in range(1, REACH + 1):
        for way in (1, -1):
            @pl.when(room(way) >= step)
            def _(way=way, step=step):
                greet(tm + way * cores * step, spot)
    greet(sibling, spot)

    @pl.when((core == 0) & (chip > 0))
    def _():
        greet(tm - 1, spot)

    @pl.when((core == 1) & (chip < chips - 1))
    def _():
        greet(tm + 1, spot)

    loads[0].wait()
    base = spot * stored

    def scan(group, carry):
        count = 0
        found = [0] * slots
        for k in range(stations):
            gap = table[k, group] - base
            hit = (gap >= 0) & (gap < stored)
            found = [jnp.where(hit & (count == n), gap, found[n]) for n in range(slots)]
            count = count + jnp.where(hit, 1, 0)
        for n in range(slots):
            picked[group % plane, (group // plane) * slots + n] = found[n]
        return carry

    lax.fori_loop(0, groups, scan, 0)
    loads[1].wait()

    row = iota((unit, channels * stored), 0)
    column = iota((unit, channels * stored), 1)

    def choose(step, carry):
        want = jnp.where(row < 2 * slots * channels, row % channels * stored, -stored)
        for n in range(2 * slots):
            want = want + jnp.where(row // channels == n, picked[step, n], 0)
        chosen[pl.ds(pl.multiple_of(step * unit, unit), unit), :] = jnp.where(column == want, 1.0, 0.0).astype(chosen.dtype)
        return carry

    lax.fori_loop(0, plane, choose, 0)
    outgoing[...] = jnp.dot(
        chosen[...], wave[...].reshape(channels * stored, samples), preferred_element_type=jnp.float32
    ).astype(outgoing.dtype).reshape(outgoing.shape)
    arrived[place] = outgoing[place]

    spots = iota((stations * channels, plane * unit), 0)
    order = iota((stations * channels, plane * unit), 1)

    def collect(group, side):
        want = spots % channels
        owners = []
        for k in range(stations):
            station = table[k, group]
            owner = station // stored
            rank = 0
            for earlier in owners:
                rank = rank + jnp.where(earlier == owner, 1, 0)
            owners.append(owner)
            place_of = owner % plane * unit + (side * slots + rank) * channels
            place_of = jnp.where(owner // plane == half, place_of, -channels)
            want = want + jnp.where(spots // channels == k, place_of, 0)
        return jnp.where(order == want, 1.0, 0.0).astype(arrived.dtype)

    across = collect(partner, 1 - half)
    local = collect(spot, half)

    loads[2].wait()
    values = raw[...].astype(jnp.float32)
    centred = values - jnp.mean(values, axis=-1, keepdims=True)
    factor = lax.rsqrt(jnp.sum(centred * centred, axis=-1, keepdims=True) + 1e-06)
    all_ref[tm] = jnp.zeros(all_ref.shape[1:], all_ref.dtype)
    all_ref[tm, :, :taps] = (centred * factor).astype(all_ref.dtype)

    peers = plane + 1
    for step in range(1, REACH + 1):
        for way in (1, -1):
            peers = peers + (room(way) + chips - step) // chips
    peers = peers + (1 - core) * ((chip + chips - 1) // chips) + core * ((2 * chips - 2 - chip) // chips)
    pl.semaphore_wait(barrier, peers)

    def row_copy(step):
        to = (place + step) % plane
        return pltpu.make_async_remote_copy(
            src_ref=outgoing.at[to], dst_ref=arrived.at[place],
            send_sem=out_sems.at[step], recv_sem=in_sems.at[step],
            device_id=(tm, half * plane + to), device_id_type=MESH,
        )

    def line_copy(way, come, go):
        window = tm - way * cores * come
        lane = (1 - way) // 2
        return pltpu.make_async_remote_copy(
            src_ref=all_ref.at[window], dst_ref=all_ref.at[window],
            send_sem=line_sends.at[lane, come + go], recv_sem=line_recvs.at[lane, come + go],
            device_id=(tm + way * cores * go, spot), device_id_type=MESH,
        )

    def side_copy(way, come):
        window = tm - way * cores * come
        lane = (1 - way) // 2
        return pltpu.make_async_remote_copy(
            src_ref=all_ref.at[window], dst_ref=all_ref.at[window],
            send_sem=side_sends.at[lane, come], recv_sem=side_recvs.at[lane, come],
            device_id=(sibling, spot), device_id_type=MESH,
        )

    def send_rows(step, carry):
        row_copy(step).start()
        return carry

    def take_rows(step, carry):
        row_copy(step).wait_recv()
        return carry

    def sent_rows(step, carry):
        row_copy(step).wait_send()
        return carry

    def send_line(go):
        for way in (1, -1):
            @pl.when(room(way) >= go)
            def _(way=way):
                line_copy(way, 0, go).start()

    send_line(HOPS[0])
    lax.fori_loop(1, plane, send_rows, 0)
    for go in range(HOPS[0] - 1, 0, -1):
        send_line(go)
    side_copy(1, 0).start()

    def receive(come):
        for way in (1, -1):
            @pl.when(room(-way) >= come)
            def _(way=way):
                line_copy(way, come, 0).wait_recv()
                if come in HOPS:
                    for go in range(HOPS[come], 0, -1):
                        @pl.when(room(way) >= go)
                        def _(go=go):
                            line_copy(way, come, go).start()
                side_copy(way, come).start()

    for come in EARLY:
        receive(come)

    tpls, nrc = lists.shape[0], stations * channels
    frames = samples // STRIDE
    padded = all_ref.shape[2]
    steps = taps // STRIDE + 1
    gap = iota((samples, LANES), 0) - STRIDE * iota((samples, LANES), 1)
    for e in range(STRIDE):
        picks[e] = jnp.where(gap == e, 1.0, 0.0).astype(picks.dtype)
    ahead = iota((2 * LANES, LANES), 0) - iota((2 * LANES, LANES), 1)
    band[...] = jnp.where((ahead >= 0) & (ahead < taps // STRIDE), 1.0, 0.0).astype(band.dtype)
    for slot in range(2):
        for c in range(channels):
            zs[slot, c, STRIDE * steps :, :] = jnp.zeros((padded - STRIDE * steps, LANES), zs.dtype)
    acc[...] = jnp.zeros_like(acc)

    loads[3].wait()
    loads[4].wait()
    who, lag = lists[...], shifts[...]
    entry = iota(who.shape, 1)
    first, late = jnp.zeros_like(who), jnp.zeros_like(who)
    for r in range(stations):
        hit = who == r
        first = jnp.where(entry == r, jnp.max(jnp.where(hit, entry, 0), axis=1, keepdims=True), first)
        late = jnp.where(entry == r, jnp.max(jnp.where(hit, lag, 0), axis=1, keepdims=True), late)
    use_pair[0] = first * channels + iota(who.shape, 0) * nrc
    use_pair[1] = late
    uses = [
        pltpu.make_async_copy(use_pair.at[n], dst, load_sems.at[5 + n]) for n, dst in enumerate((rowidx, delays))
    ]
    for use in uses:
        use.start()

    lax.fori_loop(1, plane, take_rows, 0)

    def pull(hot):
        rows = arrived[...].reshape(plane * unit, samples)
        return jnp.dot(hot, rows, preferred_element_type=jnp.float32).astype(arrived.dtype)

    cross[...] = pull(across)
    pair = pltpu.make_async_remote_copy(
        src_ref=cross, dst_ref=far_ref.at[0], send_sem=pair_sems.at[0], recv_sem=pair_sems.at[1],
        device_id=(tm, partner), device_id_type=MESH,
    )
    pair.start()
    near_ref[0] = pull(local)

    def halo(n):
        ref = (near_ref, far_ref)[n]
        return pltpu.make_async_remote_copy(
            src_ref=ref.at[0], dst_ref=ref.at[1], send_sem=halo_sems.at[n, 0], recv_sem=halo_sems.at[n, 1],
            device_id=((tm + windows - 1) % windows, spot), device_id_type=MESH,
        )

    @pl.when(tm > 0)
    def _():
        halo(0).start()

    @pl.when(tm == windows - 1)
    def _():
        near_ref[1] = jnp.zeros(near_ref.shape[1:], near_ref.dtype)
        far_ref[1] = jnp.zeros(far_ref.shape[1:], far_ref.dtype)

    lane = iota((STRIDE, LANES), 1)
    sub = iota((STRIDE, LANES), 0)

    def spread_taps(window):
        plain[...] = all_ref[window].astype(jnp.float32)

        def eight(part, carry):
            start = pl.multiple_of(part * STRIDE, STRIDE)
            for n in range(STRIDE):
                row = plain[pl.ds(start + n, 1), :]
                before = jnp.zeros((STRIDE, LANES), jnp.float32)
                for b in range(padded // LANES):
                    here = pltpu.roll(
                        jnp.broadcast_to(row[:, LANES * b : LANES * (b + 1)], (STRIDE, LANES)),
                        0, axis=1, stride=1, stride_axis=0,
                    )
                    shifted[window * nrc + start + n, :, LANES * b : LANES * (b + 1)] = jnp.where(
                        lane < sub, before, here
                    ).astype(shifted.dtype)
                    before = here
            return carry

        lax.fori_loop(0, nrc // STRIDE, eight, 0)

    def take_line(come):
        for way in (1, -1):
            @pl.when(room(-way) >= come)
            def _(way=way):
                spread_taps(tm - way * cores * come)

    def take_side(come):
        for way in (1, -1):
            @pl.when(room(-way) >= come)
            def _(way=way):
                side_copy(way, come).wait()
                spread_taps(sibling - way * cores * come)

    spread_taps(tm)
    take_line(EARLY[0])
    side_copy(1, 0).wait()
    spread_taps(sibling)
    last = EARLY[0]
    for come in ORDER:
        receive(come)
        if come == FORWARD:
            pair.wait_recv()

            @pl.when(tm > 0)
            def _():
                halo(1).start()

        take_line(come)
        take_side(last)
        last = come
    own = near_ref[0].astype(jnp.float32) + far_ref[0].astype(jnp.float32)
    own = own.astype(jnp.bfloat16)
    for e in range(STRIDE):
        xa[:, e, :] = jnp.dot(own, picks[e], preferred_element_type=jnp.float32)
    take_side(last)

    for come in HOPS:
        for go in range(1, HOPS[come] + 1):
            for way in (1, -1):
                @pl.when((room(-way) >= come) & (room(way) >= go))
                def _(way=way, come=come, go=go):
                    line_copy(way, come, go).wait_send()
    lax.fori_loop(1, plane, sent_rows, 0)
    pair.wait_send()

    @pl.when(tm < windows - 1)
    def _():
        halo(0).wait_recv()
        halo(1).wait_recv()

    @pl.when(tm > 0)
    def _():
        halo(0).wait_send()
        halo(1).wait_send()

    for use in uses:
        use.wait()
    later_rows = near_ref[1].astype(jnp.float32) + far_ref[1].astype(jnp.float32)
    later_rows = later_rows.astype(jnp.bfloat16)
    flat_lane = iota((nrc, LANES), 1)
    for e in range(STRIDE):
        phase = jnp.dot(later_rows, picks[e], preferred_element_type=jnp.float32)
        later = pltpu.roll(phase, frames, axis=1)
        xa[:, e, :] = jnp.where(flat_lane < frames, xa[:, e, :], later)
        xb[:, e, :] = later

    flat = jnp.concatenate([xa[...].reshape(nrc * STRIDE, LANES), xb[...].reshape(nrc * STRIDE, LANES)], axis=1)
    square = flat * flat
    high = square.astype(jnp.bfloat16)
    low = (square - high.astype(jnp.float32)).astype(jnp.bfloat16)

    def banded(v):
        return jnp.dot(v, band[...], preferred_element_type=jnp.float32)

    def octet(v):
        v = v.reshape(nrc, STRIDE, LANES)
        row = iota((nrc, STRIDE, LANES), 1)
        for k in (1, 2, 4):
            nxt = pltpu.roll(v, LANES - 1, axis=2)
            v = v + pltpu.roll(jnp.where(row < k, nxt, v), STRIDE - k, axis=1)
        return v

    wsum = octet(banded(flat.astype(jnp.bfloat16)))
    wsq = octet(banded(high) + banded(low))
    inv[...] = lax.rsqrt(jnp.maximum(wsq - wsum * wsum / taps, 1.0))

    lane16 = iota((2 * STRIDE, LANES), 1)
    wide = iota((nrc, STRIDE, LANES), 2)
    next_b = pltpu.roll(xb[...], LANES - 1, axis=2)
    next_a = jnp.where(wide < LANES - 1, pltpu.roll(xa[...], LANES - 1, axis=2), next_b)
    xa16[...] = jnp.concatenate([xa[...], next_a], axis=1).astype(jnp.bfloat16)
    xb16[...] = jnp.concatenate([xb[...], next_b], axis=1).astype(jnp.bfloat16)
    def build(r, slot):
        for c in range(channels):
            rc = r * channels + c
            a, b = xa16[rc], xb16[rc]
            for i in range(0, steps, 2):
                mixed = jnp.where(lane16 < i, b, a) if i else a
                zs[slot, c, STRIDE * i : STRIDE * (i + 2), :] = pltpu.roll(mixed, LANES - i, axis=1) if i else a

    def multiply(r, slot):
        products = []
        for c in range(channels):
            left = jnp.concatenate([shifted[rowidx[t, r] + c] for t in range(tpls)], axis=0)
            products.append(jnp.dot(left, zs[slot, c], preferred_element_type=jnp.float32))
        return products

    def settle(r, products):
        ratio = sum(
            products[c].reshape(tpls, STRIDE, LANES) * inv[r * channels + c][None] for c in range(channels)
        )
        for t in range(tpls):
            m = delays[t, r]
            f = m // STRIDE
            e = m - f * STRIDE
            near = pltpu.roll(ratio[t], (LANES - f) % LANES, axis=1)
            far = pltpu.roll(near, LANES - 1, axis=1)
            acc[t] += pltpu.roll(jnp.where(sub < e, far, near), (STRIDE - e) % STRIDE, axis=0)

    build(0, 0)

    def pair_of(p, carry):
        first = 2 * p
        products = multiply(first, 0)
        build(first + 1, 1)
        settle(first, products)
        products = multiply(first + 1, 1)
        build(jnp.minimum(first + 2, stations - 1), 0)
        settle(first + 1, products)
        return carry

    lax.fori_loop(0, stations // 2, pair_of, 0)

    total = acc[...].reshape(tpls * STRIDE, LANES)
    p1 = total.astype(jnp.bfloat16)
    rest = total - p1.astype(jnp.float32)
    p2 = rest.astype(jnp.bfloat16)
    p3 = (rest - p2.astype(jnp.float32)).astype(jnp.bfloat16)
    spots = iota((LANES, samples), 1) // STRIDE
    spread_out = jnp.where(spots == iota((LANES, samples), 0), 1.0, 0.0).astype(jnp.bfloat16)

    def placed(v):
        return jnp.dot(v, spread_out, preferred_element_type=jnp.float32)

    wide = (placed(p1) + placed(p2) + placed(p3)).reshape(tpls, STRIDE, samples)
    mine = iota((tpls, STRIDE, samples), 2) % STRIDE == iota((tpls, STRIDE, samples), 1)
    out_ref[...] = jnp.sum(jnp.where(mine, wide, 0.0), axis=1)


def matched_filter(table, lists, shifts, wave, tpl, slots, padded):
    windows = lax.axis_size("tm")
    cores = 2
    stations, groups = table.shape
    plane = groups // 2
    channels, stored, samples = wave.shape
    unit = -(-2 * slots * channels // 8) * 8
    nrc = stations * channels
    tpls = lists.shape[0]
    chips = windows // cores
    operands = (table, lists, shifts, wave, tpl)
    return pl.pallas_call(
        functools.partial(matched_filter_kernel, plane, cores, slots, tpl.shape[1]),
        out_shape=jax.ShapeDtypeStruct((tpls, samples), jnp.float32),
        in_specs=[pl.BlockSpec(memory_space=pltpu.HBM)] * len(operands),
        out_specs=pl.BlockSpec(memory_space=pltpu.VMEM),
        scratch_shapes=[
            pltpu.SMEM(table.shape, jnp.int32),
            pltpu.VMEM(lists.shape, jnp.int32),
            pltpu.VMEM(shifts.shape, jnp.int32),
            pltpu.VMEM(wave.shape, wave.dtype),
            pltpu.VMEM(tpl.shape, tpl.dtype),
            pltpu.SMEM((plane, 2 * slots), jnp.int32),
            pltpu.VMEM((plane * unit, channels * stored), jnp.bfloat16),
            pltpu.VMEM((plane, unit, samples), jnp.bfloat16),
            pltpu.VMEM((plane, unit, samples), jnp.bfloat16),
            pltpu.VMEM((nrc, samples), jnp.bfloat16),
            pltpu.VMEM((2, nrc, samples), jnp.bfloat16),
            pltpu.VMEM((2, nrc, samples), jnp.bfloat16),
            pltpu.VMEM((windows, tpl.shape[0], padded), jnp.bfloat16),
            pltpu.VMEM((2, *lists.shape), jnp.int32),
            pltpu.SMEM(lists.shape, jnp.int32),
            pltpu.SMEM(lists.shape, jnp.int32),
            pltpu.VMEM((STRIDE, samples, LANES), jnp.bfloat16),
            pltpu.VMEM((2 * LANES, LANES), jnp.bfloat16),
            pltpu.VMEM((nrc, padded), jnp.float32),
            pltpu.VMEM((tpls * nrc, STRIDE, padded), jnp.bfloat16),
            pltpu.VMEM((nrc, STRIDE, LANES), jnp.float32),
            pltpu.VMEM((nrc, STRIDE, LANES), jnp.float32),
            pltpu.VMEM((nrc, STRIDE, LANES), jnp.float32),
            pltpu.VMEM((nrc, 2 * STRIDE, LANES), jnp.bfloat16),
            pltpu.VMEM((nrc, 2 * STRIDE, LANES), jnp.bfloat16),
            pltpu.VMEM((2, channels, padded, LANES), jnp.bfloat16),
            pltpu.VMEM((tpls, STRIDE, LANES), jnp.float32),
            pltpu.SemaphoreType.DMA((7,)),
            pltpu.SemaphoreType.DMA((plane,)),
            pltpu.SemaphoreType.DMA((plane,)),
            pltpu.SemaphoreType.DMA((2,)),
            pltpu.SemaphoreType.DMA((2, 2)),
            pltpu.SemaphoreType.DMA((2, chips)),
            pltpu.SemaphoreType.DMA((2, chips)),
            pltpu.SemaphoreType.DMA((2, chips)),
            pltpu.SemaphoreType.DMA((2, chips)),
        ],
        compiler_params=pltpu.CompilerParams(
            collective_id=0, has_side_effects=True, vmem_limit_bytes=40 << 20
        ),
    )(*(pltpu.with_memory_space_constraint(v, pltpu.HBM) for v in operands))


def per_device(waveforms, templates, group_stations, template_rows, moveouts):
    slots = max(2, 2 * group_stations.shape[1] // lax.axis_size("tmpl"))
    padded = (templates.shape[3] + LANES - 1) // LANES * LANES
    return matched_filter(
        group_stations.T, template_rows[0], moveouts[0], waveforms.transpose(1, 0, 2), templates[0, 0], slots, padded
    )[None]


def solution(mesh):
    in_specs = (
        P("tmpl", None, "tm"),
        P("tmpl", "tm", None, None),
        P(),
        P("tmpl", None, None),
        P("tmpl", None, None),
    )
    out_specs = P("tmpl", None, "tm")
    return jax.shard_map(
        per_device, mesh=mesh, in_specs=in_specs, out_specs=out_specs, check_vma=False
    )
```
